128 devices in a mesh: clip: 16 (over z, x), patch: 8 (over y, core).
Axes of the slice: x: 4, y: 4, z: 4, core: 2. Of those that a mesh axis runs over, the one named last changes fastest.
Arguments:
- pixels: bfloat16 [1024, 16, 64, 384], P(('clip', 'patch')), may hold values from -40 to 40
- destination: int32 [1024, 1], P(('clip', 'patch')), may hold values from 0 to 15; in each aligned block of 8 rows (0 to 7, 8 to 15, ...) at most 2 rows name the same one
- embed_weight: bfloat16 [384, 128], replicated, may hold values from -0.3125 to 0.3125
- embed_gain: float32 [128], replicated, may hold values from 0.5 to 2
- mixing_weight: bfloat16 [9, 384, 256], replicated, may hold values from -0.109375 to 0.109375
- mixing_gain: float32 [256], replicated, may hold values from 0.5 to 2
- project_weight: bfloat16 [256, 512], replicated, may hold values from -0.375 to 0.375
- project_gain: float32 [512], replicated, may hold values from 0.25 to 1.75
Outputs:
- latents: bfloat16 [4096, 8, 64, 512], P('clip', None, 'patch')
The draws below stay inside these ranges and needn't reach their ends.
Inputs may be any that keep to these rules, and one draw needn't show every extreme that they name: `destination`: among the 8 clips of one owner device (aligned blocks of 8 rows) no tokenizer index occurs more than 2 times, and some index occurs exactly 2 times in some blocks.
All inputs are finite; a program needn't handle non-finite values.
Results may differ from the reference program's by a relative error of at most 0.0059.
Values may be sent and summed in bfloat16 or wider, within the bound.
A program may use at most 128 MiB of HBM per device.

```python
import math
import jax
import jax.numpy as jnp
import numpy as np
from jax import lax

GRID = 8
TUBE = 384
C1 = 128
C2 = 256
C3 = 512
GROUPS = 32
CAP = 2
LT1 = 16
LT2 = 8
POS = 64
OWN = 8
CLIPS = 1024
SLOTS = 4096
N_CLIP = 16
N_PATCH = 8


def draw_pixels(key, part):
    first, second, third = jax.random.split(key, 3)
    shape = (CLIPS, LT1, POS, TUBE)
    row_scale = jnp.exp(jax.random.uniform(second, (CLIPS, LT1, POS, 1), jnp.float32, 0.0, math.log(10.0)))
    col_scale = jnp.exp(jax.random.uniform(third, (CLIPS, 1, 1, TUBE), jnp.float32, 0.0, math.log(10.0)))
    base = jnp.clip(jax.random.normal(first, shape, jnp.float32), -4.0, 4.0)
    return (0.1 * base * row_scale * col_scale).astype(jnp.bfloat16)


def assign_block(rng, own, number, rows, number_of, top, most, lean):
    sequence = jax.random.permutation(rng, number_of)
    packed, common = portions_of(number_of, rows * top, most, lean, True), portions_of(number_of, rows * top, most, lean, False)
    places = jnp.arange(number_of)

    def named(lengths, turn):
        used = int((lengths > 0).sum())
        fixed = max(1, used // 4)
        passed = fixed + (places - fixed + turn * (used - fixed)) % max(1, number_of - fixed)
        return jnp.zeros((number_of,), jnp.int32).at[sequence[jnp.where(places < fixed, places, passed)]].set(jnp.asarray(lengths, jnp.int32))

    lengths = jnp.where(number % 4 == 0, named(packed, number // 4), named(common, number - number // 4 - 1))
    mixed = jax.random.permutation(jax.random.fold_in(own, 3), number_of)
    source_of, receiver = mixed[0:number_of // 2 * 2:2], mixed[1:number_of // 2 * 2:2]
    slack = jnp.minimum(lengths[source_of] - 1, most - lengths[receiver]) // 2
    slack = jnp.where((source_of == sequence[0]) | (receiver == sequence[0]) | (lengths[receiver] == 0), 0, jnp.maximum(slack, 0))
    passed = jax.random.randint(jax.random.fold_in(own, 4), (number_of // 2,), 0, 1 << 20) % (slack + 1)
    lengths = lengths.at[source_of].add(-passed).at[receiver].add(passed)
    labels = jnp.searchsorted(jnp.cumsum(lengths), jnp.arange(rows * top), side="right").astype(jnp.int32)
    listing = labels.reshape(top, rows).T
    listing = listing[jax.random.permutation(jax.random.fold_in(own, 1), rows)]
    turn = jax.random.randint(jax.random.fold_in(own, 2), (rows, 1), 0, top)
    return jnp.take_along_axis(listing, (jnp.arange(top)[None, :] + turn) % top, axis=1)


def portions_of(amount, total, most, slope, full):
    weights = [(1 << 20) // math.isqrt(rank ** slope) + 1 for rank in range(1, amount + 1)]
    largest = most if full else min(most, max(-(-total // amount), total * weights[0] // sum(weights)))
    least = 1 if total - largest >= amount - 1 else 0
    counts, spare = [largest] + [least] * (amount - 1), total - largest - least * (amount - 1)
    while spare > 0:
        free = [i for i in range(1, amount) if counts[i] < largest] or [i for i in range(1, amount) if counts[i] < most]
        mass, budget = sum([weights[i] for i in free]), spare
        for i in free:
            extra = min(most - counts[i], max(1, budget * weights[i] // mass), spare)
            counts[i] = counts[i] + extra
            spare = spare - extra
    return np.array(counts)


def gaussian(stream_key, dims, deviation, limit, held_as=jnp.bfloat16):
    return jnp.clip(deviation * jax.random.normal(stream_key, dims, jnp.float32), -limit, limit).astype(held_as)


def setup_inputs(seed: int = 0) -> dict:
    streams_of = jax.random.split(jax.random.key(seed), 9)
    pixels = draw_pixels(jax.random.fold_in(streams_of[8], 71), 0)
    destination_keys = jax.random.split(jax.random.fold_in(streams_of[1], 1), CLIPS // OWN)
    destination_turns = jax.random.permutation(jax.random.fold_in(streams_of[1], 3), CLIPS // OWN)
    destination = jax.vmap(lambda own, number: assign_block(jax.random.fold_in(streams_of[1], 2), own, number, OWN, N_CLIP, 1, CAP, 2))(destination_keys, destination_turns).reshape((CLIPS, 1))
    embed_weight = gaussian(streams_of[2], (TUBE, C1), TUBE ** -0.5, 0.3125)
    embed_gain = jnp.clip(jnp.exp(jax.random.uniform(streams_of[3], (C1,), jnp.float32, math.log(0.5), math.log(2.0))), 0.5, 2.0)
    mixing_weight = gaussian(streams_of[4], (9, 3 * C1, C2), (27 * C1) ** -0.5, 0.109375)
    mixing_gain = jnp.clip(jnp.exp(jax.random.uniform(streams_of[5], (C2,), jnp.float32, math.log(0.5), math.log(2.0))), 0.5, 2.0)
    project_weight = gaussian(streams_of[6], (C2, C3), C2 ** -0.5, 0.375)
    project_gain = jnp.clip(1.0 + 0.15 * jax.random.normal(streams_of[7], (C3,), jnp.float32), 0.25, 1.75)
    return {"pixels": pixels, "destination": destination, "embed_weight": embed_weight, "embed_gain": embed_gain, "mixing_weight": mixing_weight, "mixing_gain": mixing_gain, "project_weight": project_weight, "project_gain": project_gain}


def group_norm(values, scales):
    number, frames, places, channels = values.shape
    grouped = values.reshape(number, frames, places, GROUPS, channels // GROUPS)
    average = lax.optimization_barrier(jnp.mean(grouped, axis=(1, 2, 4), keepdims=True))
    centred = grouped - average
    spread = lax.optimization_barrier(jnp.mean(centred * centred, axis=(1, 2, 4), keepdims=True))
    return (centred * lax.rsqrt(spread + 1e-05)).reshape(number, frames, places, channels) * scales

def encode(tubes, embed_weight, embed_gain, mixing_weight, mixing_gain, project_weight, project_gain):
    number, frames, places, breadth = tubes.shape
    embedded = jnp.dot(tubes.reshape(-1, breadth), embed_weight, preferred_element_type=jnp.float32)
    embedded = embedded.reshape(number, frames, places, -1)
    first_act = jax.nn.silu(group_norm(embedded, embed_gain)).astype(jnp.bfloat16)
    channels = first_act.shape[-1]
    padded = jnp.concatenate([jnp.zeros((number, 1, places, channels), jnp.bfloat16), first_act], axis=1)
    latent_frames = frames // 2
    stacked = jnp.concatenate([padded[:, time_tap:time_tap + 2 * latent_frames - 1:2] for time_tap in range(3)], axis=-1)
    stacked = stacked.reshape(number, latent_frames, GRID, GRID, 3 * channels)
    stacked = jnp.pad(stacked, ((0, 0), (0, 0), (1, 1), (1, 1), (0, 0)))
    summed = jnp.zeros((number * latent_frames * places, mixing_weight.shape[-1]), jnp.float32)
    for row_tap in range(3):
        for col_tap in range(3):
            window = stacked[:, :, row_tap:row_tap + GRID, col_tap:col_tap + GRID].reshape(-1, 3 * channels)
            summed = summed + jnp.dot(window, mixing_weight[row_tap * 3 + col_tap], preferred_element_type=jnp.float32)
    second = summed.reshape(number, latent_frames, places, -1)
    second_act = jax.nn.silu(group_norm(second, mixing_gain)).astype(jnp.bfloat16)
    projected = jnp.dot(second_act.reshape(-1, second_act.shape[-1]), project_weight, preferred_element_type=jnp.float32)
    projected = projected.reshape(number, latent_frames, places, -1)
    return group_norm(projected, project_gain).astype(jnp.bfloat16)

def reference(pixels, destination, embed_weight, embed_gain, mixing_weight, mixing_gain, project_weight, project_gain):
    owners = N_CLIP * N_PATCH
    targets = destination.reshape(owners, OWN)
    same = targets[:, :, None] == targets[:, None, :]
    order = jnp.arange(OWN, dtype=jnp.int32)
    earlier = order[:, None] > order[None, :]
    ranks = lax.optimization_barrier(jnp.sum((same & earlier[None]).astype(jnp.int32), axis=2)).astype(jnp.int32)
    owner_ids = jnp.arange(owners, dtype=jnp.int32)[:, None]
    slots = targets * (N_PATCH * N_CLIP * CAP) + owner_ids % N_PATCH * (N_CLIP * CAP) + owner_ids // N_PATCH * CAP + ranks

    def one_owner(block):
        return encode(block, embed_weight, embed_gain, mixing_weight, mixing_gain, project_weight, project_gain)
    encoded = lax.map(one_owner, pixels.reshape(owners, OWN, LT1, POS, TUBE))
    latents = jnp.zeros((SLOTS, LT2, POS, C3), jnp.bfloat16)
    return latents.at[slots.reshape(-1)].set(encoded.reshape(-1, LT2, POS, C3))
```

```python
import functools

import jax
import jax.numpy as jnp
from jax import lax
from jax.experimental import pallas as pl
from jax.experimental.pallas import tpu as pltpu
from jax.sharding import PartitionSpec as P

GRID = 8
CAP = 2
OWN = 8
C1, C2, C3 = 128, 256, 512
GROUPS = 32
PAIR = 2
HI = lax.Precision.HIGHEST


def fold(rows, size):
    lanes = rows.shape[1]
    lane = lax.broadcasted_iota(jnp.int32, rows.shape, 1)
    step = 1
    while step < size:
        up = pltpu.roll(rows, lanes - step, 1)
        down = pltpu.roll(rows, step, 1)
        rows = rows + jnp.where((lane & step) == 0, up, down)
        step *= 2
    return rows


def group_sums(parts):
    channels = parts[0].shape[1]
    size = channels // GROUPS
    rows = []
    for part in parts:
        total = jnp.sum(part, axis=0, keepdims=True)
        rows += [total[:, i : i + 128] for i in range(0, channels, 128)]
    folded = fold(jnp.concatenate(rows, axis=0), size)
    each = channels // 128
    return [
        jnp.concatenate([folded[n * each + i : n * each + i + 1] for i in range(each)], axis=1)
        for n in range(len(parts))
    ]


def moments(parts):
    rows, channels = parts[0].shape
    inverse = 1.0 / (rows * (channels // GROUPS))
    means = [s * inverse for s in group_sums(parts)]
    squares = []
    for part, mean in zip(parts, means):
        centred = part - mean
        squares.append(centred * centred)
    scales = [lax.rsqrt(s * inverse + 1e-05) for s in group_sums(squares)]
    return means, scales


def silu(v):
    h = 0.5 * v
    return h + h * jnp.tanh(h)


def encode_pair(tubes, embed_w, embed_g, mixing_w, mixing_g, project_w, spread, act_refs):
    first = [jnp.dot(t, embed_w[...], preferred_element_type=jnp.float32) for t in tubes]
    means, scales = moments(first)
    for n in range(PAIR):
        act = silu((first[n] - means[n]) * (scales[n] * embed_g[...]))
        act = act.reshape(8, 2, GRID, GRID, C1)
        even, odd = act[:, 0], act[:, 1]
        place = lax.broadcasted_iota(jnp.int32, (8 * GRID * GRID, C1), 0) % GRID
        for j in range(3):
            for a, source in ((1, even), (2, odd)):
                flat = source.reshape(8 * GRID * GRID, C1)
                moved = source
                if j == 0:
                    moved = jnp.where(place == 0, 0.0, pltpu.roll(flat, 1, 0))
                elif j == 2:
                    moved = jnp.where(place == GRID - 1, 0.0, pltpu.roll(flat, 8 * GRID * GRID - 1, 0))
                moved = moved.reshape(8, GRID, GRID, C1)
                low = (j * 3 + a) * C1
                for y in range(GRID):
                    block = moved[:, y].reshape(64, C1)
                    spread[n, y, :, low : low + C1] = block.astype(jnp.bfloat16)
                    if a == 2:
                        prior = jnp.concatenate([jnp.zeros((GRID, C1), jnp.float32), block[:-GRID]], axis=0)
                        spread[n, y, :, low - 2 * C1 : low - C1] = prior.astype(jnp.bfloat16)
    second = []
    for n in range(PAIR):
        mid = jnp.dot(spread[n].reshape(512, 9 * C1), mixing_w[1], preferred_element_type=jnp.float32)
        low = jnp.dot(spread[n, 0:7].reshape(448, 9 * C1), mixing_w[0], preferred_element_type=jnp.float32)
        high = jnp.dot(spread[n, 1:8].reshape(448, 9 * C1), mixing_w[2], preferred_element_type=jnp.float32)
        none = jnp.zeros((64, C2), jnp.float32)
        second.append(
            mid + jnp.concatenate([none, low], axis=0) + jnp.concatenate([high, none], axis=0)
        )
    means, scales = moments(second)
    projected = []
    for n in range(PAIR):
        act = silu((second[n] - means[n]) * (scales[n] * mixing_g[...])).astype(jnp.bfloat16)
        act_refs[n][...] = act.reshape(GRID, 64, C2)
        projected.append(jnp.dot(act, project_w[...], preferred_element_type=jnp.float32))
    return moments(projected)


def pick_lanes(mean, scale):
    channel = lax.broadcasted_iota(jnp.int32, (C3, 128), 0)
    lane = lax.broadcasted_iota(jnp.int32, (C3, 128), 1)
    of_mean = ((channel == lane * 16) & (lane < 32)).astype(jnp.float32)
    of_scale = ((channel == (lane - 32) * 16) & (lane >= 32) & (lane < 64)).astype(jnp.float32)
    return jnp.dot(mean, of_mean, precision=HI, preferred_element_type=jnp.float32) + jnp.dot(
        scale, of_scale, precision=HI, preferred_element_type=jnp.float32
    )


def encode_kernel(
    slots, pixels, embed_w, embed_g, mixing_w, mixing_g, project_w, out, stats, spread, act, mean_s, scale_s, sems
):
    step = pl.program_id(0)
    steps = OWN // PAIR
    half = lax.rem(step, 2)

    def copies(at, buffer):
        return [
            pltpu.make_async_copy(
                act.at[buffer, n],
                out.at[slots[PAIR * at + n] // CAP, :, lax.rem(slots[PAIR * at + n], CAP)],
                sems.at[buffer, n],
            )
            for n in range(PAIR)
        ]

    @pl.when(step >= 2)
    def _():
        for copy in copies(step - 2, half):
            copy.wait()

    tubes = [pixels[n].reshape(1024, 384) for n in range(PAIR)]
    means, scales = encode_pair(
        tubes, embed_w, embed_g, mixing_w, mixing_g, project_w, spread, [act.at[half, n] for n in range(PAIR)]
    )
    for copy in copies(step, half):
        copy.start()
    for n in range(PAIR):
        mean_s[step, n : n + 1] = means[n]
        scale_s[step, n : n + 1] = scales[n]

    @pl.when(step == steps - 1)
    def _():
        mean = mean_s[:, 0:PAIR].reshape(OWN, C3)
        scale = scale_s[:, 0:PAIR].reshape(OWN, C3)
        stats[...] = pick_lanes(mean, scale)
        for at in (steps - 2, steps - 1):
            for copy in copies(at, at % 2):
                copy.wait()


def encode_call(slots, pixels, embed_w, embed_g, mixing_w, mixing_g, project_w):
    whole = lambda *shape: pl.BlockSpec(shape, lambda i, s: (0,) * len(shape), pipeline_mode=pl.Buffered(1))
    return pl.pallas_call(
        encode_kernel,
        grid_spec=pltpu.PrefetchScalarGridSpec(
            num_scalar_prefetch=1,
            grid=(OWN // PAIR,),
            in_specs=[
                pl.BlockSpec((PAIR, 16, 64, 384), lambda i, s: (i, 0, 0, 0)),
                whole(384, C1),
                whole(1, C1),
                whole(3, 9 * C1, C2),
                whole(1, C2),
                whole(C2, C3),
            ],
            out_specs=[pl.BlockSpec(memory_space=pl.ANY), whole(OWN, 128)],
            scratch_shapes=[
                pltpu.VMEM((PAIR, GRID, 64, 9 * C1), jnp.bfloat16),
                pltpu.VMEM((2, PAIR, GRID, 64, C2), jnp.bfloat16),
                pltpu.VMEM((OWN // PAIR, PAIR, C3), jnp.float32),
                pltpu.VMEM((OWN // PAIR, PAIR, C3), jnp.float32),
                pltpu.SemaphoreType.DMA((2, PAIR)),
            ],
        ),
        out_shape=[
            jax.ShapeDtypeStruct((16, GRID, CAP, 64, C2), jnp.bfloat16),
            jax.ShapeDtypeStruct((OWN, 128), jnp.float32),
        ],
        compiler_params=pltpu.CompilerParams(vmem_limit_bytes=60 * 2**20),
        name="encode",
    )(slots, pixels, embed_w, embed_g, mixing_w, mixing_g, project_w)


def decode_kernel(act, stats, weight, gain, out):
    group = lax.broadcasted_iota(jnp.int32, (128, C3), 1) // 16
    lane = lax.broadcasted_iota(jnp.int32, (128, C3), 0)
    st = stats[...]
    mean = jnp.dot(st, (lane == group).astype(jnp.float32), precision=HI, preferred_element_type=jnp.float32)
    scale = jnp.dot(st, (lane == group + 32).astype(jnp.float32), precision=HI, preferred_element_type=jnp.float32)
    scale = scale * gain[...]
    taken = jnp.broadcast_to(st[:, 64:65], mean.shape) > 0.5
    rows = act[...].reshape(-1, C2)
    values = jnp.dot(rows, weight[...], preferred_element_type=jnp.float32).reshape(-1, 64, C3)
    values = (values - mean[:, None, :]) * scale[:, None, :]
    out[...] = jnp.where(taken[:, None, :], values, 0.0).astype(jnp.bfloat16)


def decode_call(act, stats, weight, gain):
    return pl.pallas_call(
        decode_kernel,
        grid=(16,),
        in_specs=[
            pl.BlockSpec((8, None, CAP, 64, C2), lambda i: (i % 2, i // 2, 0, 0, 0)),
            pl.BlockSpec((16, 128), lambda i: (i, 0)),
            pl.BlockSpec((C2, C3), lambda i: (0, 0)),
            pl.BlockSpec((1, C3), lambda i: (0, 0)),
        ],
        out_specs=pl.BlockSpec((16, 64, C3), lambda i: (i, 0, 0)),
        out_shape=jax.ShapeDtypeStruct((256, 64, C3), jnp.bfloat16),
        compiler_params=pltpu.CompilerParams(vmem_limit_bytes=60 * 2**20),
        name="decode",
    )(act, stats, weight, gain)


def ranks_of(targets):
    order = jnp.arange(OWN, dtype=jnp.int32)
    same = targets[..., :, None] == targets[..., None, :]
    return jnp.sum((same & (order[:, None] > order[None, :])).astype(jnp.int32), axis=-1)


def on_device(
    pixels, destination, embed_weight, embed_gain, mixing_weight, mixing_gain, project_weight, project_gain
):
    targets = destination[:, 0]
    slots = targets * CAP + ranks_of(targets)
    outgoing, stats = encode_call(
        slots,
        pixels,
        embed_weight,
        embed_gain.reshape(1, C1),
        mixing_weight.reshape(3, 9 * C1, C2),
        mixing_gain.reshape(1, C2),
        project_weight,
    )
    arrived = lax.all_to_all(
        outgoing.reshape(128, CAP, 64, C2), ("clip", "patch"), split_axis=0, concat_axis=0, tiled=True
    )
    everyone = lax.all_gather(targets, ("clip", "patch"), axis=0)
    stats = lax.all_gather(stats, ("clip", "patch"), axis=0)
    rank = ranks_of(everyone)
    mine = everyone == lax.axis_index("clip")
    match = (mine[:, None, :] & (rank[:, None, :] == jnp.arange(CAP)[None, :, None])).astype(jnp.float32)
    stats = jnp.sum(match[..., None] * stats[:, None], axis=2)
    lane = jnp.arange(128)
    stats = jnp.where(lane == 64, jnp.sum(match, axis=2)[..., None], stats)
    stats = stats.reshape(16, GRID, CAP, 128).transpose(1, 0, 2, 3).reshape(256, 128)
    out = decode_call(
        arrived.reshape(16, GRID, CAP, 64, C2), stats, project_weight, project_gain.reshape(1, C3)
    )
    return out.reshape(256, 8, GRID, C3)


def solution(mesh):
    return jax.shard_map(
        on_device,
        mesh=mesh,
        in_specs=(P(("clip", "patch"), None, None, None), P(("clip", "patch"), None), P(), P(), P(), P(), P(), P()),
        out_specs=P("clip", None, "patch", None),
        check_vma=False,
    )
```

```python
import functools

import jax
import jax.numpy as jnp
from jax import lax
from jax.experimental import pallas as pl
from jax.experimental.pallas import tpu as pltpu
from jax.sharding import PartitionSpec as P

GRID = 8
CAP = 2
OWN = 8
C1, C2, C3 = 128, 256, 512
GROUPS = 32
PAIR = 2
SIDE = 4
STEPS = OWN // PAIR
HI = lax.Precision.HIGHEST
MESH = pl.DeviceIdType.MESH


def fold(rows, size):
    lanes = rows.shape[1]
    lane = lax.broadcasted_iota(jnp.int32, rows.shape, 1)
    step = 1
    while step < size:
        up = pltpu.roll(rows, lanes - step, 1)
        down = pltpu.roll(rows, step, 1)
        rows = rows + jnp.where((lane & step) == 0, up, down)
        step *= 2
    return rows


def group_sums(parts):
    channels = parts[0].shape[1]
    size = channels // GROUPS
    rows = []
    for part in parts:
        total = jnp.sum(part, axis=0, keepdims=True)
        rows += [total[:, i : i + 128] for i in range(0, channels, 128)]
    folded = fold(jnp.concatenate(rows, axis=0), size)
    each = channels // 128
    return [
        jnp.concatenate([folded[n * each + i : n * each + i + 1] for i in range(each)], axis=1)
        for n in range(len(parts))
    ]


def moments(parts):
    rows, channels = parts[0].shape
    inverse = 1.0 / (rows * (channels // GROUPS))
    means = [s * inverse for s in group_sums(parts)]
    squares = []
    for part, mean in zip(parts, means):
        centred = part - mean
        squares.append(centred * centred)
    scales = [lax.rsqrt(s * inverse + 1e-05) for s in group_sums(squares)]
    return means, scales


def silu(v):
    h = 0.5 * v
    return h + h * jnp.tanh(h)


def encode_pair(tubes, embed_w, embed_g, mixing_w, mixing_g, project_w, spread, act, after):
    first = [jnp.dot(t, embed_w[...], preferred_element_type=jnp.float32) for t in tubes]
    means, scales = moments(first)
    for n in range(PAIR):
        wide = silu((first[n] - means[n]) * (scales[n] * embed_g[...]))
        wide = wide.reshape(8, 2, GRID, GRID, C1)
        even, odd = wide[:, 0], wide[:, 1]
        place = lax.broadcasted_iota(jnp.int32, (8 * GRID * GRID, C1), 0) % GRID
        for j in range(3):
            for a, source in ((1, even), (2, odd)):
                flat = source.reshape(8 * GRID * GRID, C1)
                moved = source
                if j == 0:
                    moved = jnp.where(place == 0, 0.0, pltpu.roll(flat, 1, 0))
                elif j == 2:
                    moved = jnp.where(place == GRID - 1, 0.0, pltpu.roll(flat, 8 * GRID * GRID - 1, 0))
                moved = moved.reshape(8, GRID, GRID, C1)
                low = (j * 3 + a) * C1
                for y in range(GRID):
                    block = moved[:, y].reshape(64, C1)
                    spread[n, y, :, low : low + C1] = block.astype(jnp.bfloat16)
                    if a == 2:
                        prior = jnp.concatenate([jnp.zeros((GRID, C1), jnp.float32), block[:-GRID]], axis=0)
                        spread[n, y, :, low - 2 * C1 : low - C1] = prior.astype(jnp.bfloat16)
    second = []
    for n in range(PAIR):
        mid = jnp.dot(spread[n].reshape(512, 9 * C1), mixing_w[1], preferred_element_type=jnp.float32)
        low = jnp.dot(spread[n, 0:7].reshape(448, 9 * C1), mixing_w[0], preferred_element_type=jnp.float32)
        high = jnp.dot(spread[n, 1:8].reshape(448, 9 * C1), mixing_w[2], preferred_element_type=jnp.float32)
        none = jnp.zeros((64, C2), jnp.float32)
        second.append(
            mid + jnp.concatenate([none, low], axis=0) + jnp.concatenate([high, none], axis=0)
        )
    means, scales = moments(second)
    acts = []
    for n in range(PAIR):
        acts.append(silu((second[n] - means[n]) * (scales[n] * mixing_g[...])).astype(jnp.bfloat16))
        act[:, n] = acts[n].reshape(GRID, 64, C2)
    after()
    return moments([jnp.dot(a, project_w[...], preferred_element_type=jnp.float32) for a in acts])


def pick_lanes(mean, scale):
    channel = lax.broadcasted_iota(jnp.int32, (C3, 128), 0)
    lane = lax.broadcasted_iota(jnp.int32, (C3, 128), 1)
    of_mean = ((channel == lane * 16) & (lane < 32)).astype(jnp.float32)
    of_scale = ((channel == (lane - 32) * 16) & (lane >= 32) & (lane < 64)).astype(jnp.float32)
    return jnp.dot(mean, of_mean, precision=HI, preferred_element_type=jnp.float32) + jnp.dot(
        scale, of_scale, precision=HI, preferred_element_type=jnp.float32
    )


class Place:
    def __init__(self):
        self.c, self.p = lax.axis_index("clip"), lax.axis_index("patch")
        self.z, self.x = self.c // SIDE, lax.rem(self.c, SIDE)

    def line(self, which):
        return self.z if which else self.x

    def beside(self, which, by):
        other = lax.rem(self.line(which) + by, SIDE)
        return (other * SIDE + self.x if which else self.z * SIDE + other, self.p), other

    def partner(self, by):
        other = lax.rem(self.p + by, GRID)
        return (self.c, other), other


def encode_kernel(
    order, pixels, embed_w, embed_g, mixing_w, mixing_g, project_w, extra,
    own, wide_x, wide_z, stats,
    tubes, spread, act, mean_s, scale_s, tile, pix_sem, send_y, recv_y, keep_y, send_g, recv_g, send_f, recv_f, send_s,
    recv_s, keep_s,
):
    me = Place()
    wide = (wide_x, wide_z)
    loads = [pltpu.make_async_copy(pixels.at[n], tubes.at[n], pix_sem.at[n]) for n in range(OWN)]
    for load in loads:
        load.start()
    barrier = pltpu.get_barrier_semaphore()
    for by in range(1, GRID):
        pl.semaphore_signal(barrier, inc=1, device_id=me.partner(by)[0], device_id_type=MESH)
    for which in range(2):
        for by in range(1, SIDE):
            pl.semaphore_signal(barrier, inc=1, device_id=me.beside(which, by)[0], device_id_type=MESH)
    pl.semaphore_wait(barrier, GRID - 1 + 2 * (SIDE - 1))
    for load in loads:
        load.wait()

    def remote(src, dst, send, recv, device):
        return pltpu.make_async_remote_copy(
            src_ref=src, dst_ref=dst, send_sem=send, recv_sem=recv, device_id=device, device_id_type=MESH
        )

    def across(m, by):
        device, other = me.partner(by)
        return remote(act.at[m, other], own.at[m, me.p], send_y.at[m, by], recv_y.at[m, me.p], device)

    def across_in(m, by):
        device, other = me.partner(by)
        return remote(act.at[m, other], own.at[m, other], send_y.at[m, by], recv_y.at[m, other], device)

    def kept(m):
        return pltpu.make_async_copy(act.at[m, me.p], own.at[m, me.p], keep_y.at[m])

    def gather(which, m, way):
        device, _ = me.beside(which, 1 if way == 0 else SIDE - 1)
        return remote(
            own.at[m, :, which], wide[which].at[me.line(which), m], send_g.at[which, m, way], recv_g.at[which, m, way], device
        )

    def gather_in(which, m, way):
        device, other = me.beside(which, SIDE - 1 if way == 0 else 1)
        return remote(
            own.at[m, :, which], wide[which].at[other, m], send_g.at[which, m, way], recv_g.at[which, m, way], device
        )

    def half(which, line, m, way):
        return wide[which].at[line, m, pl.ds(way * 4, 4)]

    def pass_on(which, m, way):
        _, origin = me.beside(which, SIDE - 1 if way == 0 else 1)
        device, _ = me.beside(which, 1 if way == 0 else SIDE - 1)
        part = half(which, origin, m, way)
        return remote(part, part, send_f.at[which, m, way], recv_f.at[which, m, way], device)

    def pass_on_in(which, m, way):
        device, origin = me.beside(which, 2)
        part = half(which, origin, m, way)
        return remote(part, part, send_f.at[which, m, way], recv_f.at[which, m, way], device)

    both = [(which, way) for which in range(2) for way in range(2)]

    def start_across(m):
        for by in range(1, GRID):
            across(m, by).start()
        kept(m).start()

    def start_gather(m):
        kept(m).wait()
        for by in range(1, GRID):
            across_in(m, by).wait_recv()
        for which, way in both:
            gather(which, m, way).start()

    def start_pass(m):
        for which, way in both:
            gather_in(which, m, way).wait_recv()
            pass_on(which, m, way).start()

    def encode(m):
        def after():
            @pl.when(m >= 1)
            def _():
                start_gather(m - 1)

            start_across(m)

            @pl.when(m >= 2)
            def _():
                start_pass(m - 2)

        values = [tubes[order[PAIR * m + n]].reshape(1024, 384) for n in range(PAIR)]
        means, scales = encode_pair(
            values, embed_w, embed_g, mixing_w, mixing_g, project_w, spread, act.at[m], after
        )
        for n in range(PAIR):
            mean_s[m, n : n + 1] = means[n]
            scale_s[m, n : n + 1] = scales[n]

    def stat_y(by, incoming):
        device, other = me.partner(by)
        at = other if incoming else me.p
        return remote(tile, stats.at[me.c, at], send_s.at[by], recv_s.at[0, at], device)

    def stat_x(by, incoming):
        device, other = me.beside(0, by)
        row = stats.at[me.z * SIDE + (other if incoming else me.x)]
        return remote(stats.at[me.c], row, send_s.at[GRID + by], recv_s.at[1, other if incoming else me.x], device)

    def stat_z(by, incoming):
        device, other = me.beside(1, by)
        mine = stats.at[pl.ds(me.z * SIDE, SIDE)]
        rows = stats.at[pl.ds((other if incoming else me.z) * SIDE, SIDE)]
        return remote(mine, rows, send_s.at[GRID + SIDE + by], recv_s.at[2, other if incoming else me.z], device)

    def loop(m, carry):
        encode(m)
        return carry

    lax.fori_loop(0, STEPS, loop, 0)
    mean = mean_s[...].reshape(OWN, C3)
    scale = scale_s[...].reshape(OWN, C3)
    tile[...] = pick_lanes(mean, scale) + extra[...]
    for by in range(1, GRID):
        stat_y(by, False).start()
    keep = pltpu.make_async_copy(tile, stats.at[me.c, me.p], keep_s.at[0])
    keep.start()
    start_gather(STEPS - 1)
    start_pass(STEPS - 2)
    keep.wait()
    for by in range(1, GRID):
        stat_y(by, True).wait_recv()
    for by in range(1, SIDE):
        stat_x(by, False).start()
    for by in range(1, SIDE):
        stat_x(by, True).wait_recv()
    for by in range(1, SIDE):
        stat_z(by, False).start()
    start_pass(STEPS - 1)

    def drain(m, carry):
        for by in range(1, GRID):
            across(m, by).wait_send()
        for which, way in both:
            gather(which, m, way).wait_send()
            pass_on_in(which, m, way).wait_recv()
            pass_on(which, m, way).wait_send()
        return carry

    lax.fori_loop(0, STEPS, drain, 0)
    for by in range(1, SIDE):
        stat_z(by, True).wait_recv()
    for by in range(1, GRID):
        stat_y(by, False).wait_send()
    for by in range(1, SIDE):
        stat_x(by, False).wait_send()
        stat_z(by, False).wait_send()


def encode_call(order, pixels, embed_w, embed_g, mixing_w, mixing_g, project_w, extra):
    anywhere = pl.BlockSpec(memory_space=pl.ANY)
    inside = pl.BlockSpec(memory_space=pltpu.VMEM)
    dma = pltpu.SemaphoreType.DMA
    return pl.pallas_call(
        encode_kernel,
        in_specs=[pl.BlockSpec(memory_space=pltpu.SMEM), anywhere] + [inside] * 6,
        out_specs=[anywhere] * 4,
        out_shape=[
            jax.ShapeDtypeStruct((STEPS, GRID, PAIR, 64, C2), jnp.bfloat16),
            jax.ShapeDtypeStruct((SIDE, STEPS, GRID, 64, C2), jnp.bfloat16),
            jax.ShapeDtypeStruct((SIDE, STEPS, GRID, 64, C2), jnp.bfloat16),
            jax.ShapeDtypeStruct((SIDE * SIDE, GRID, OWN, 128), jnp.float32),
        ],
        scratch_shapes=[
            pltpu.VMEM((OWN, 16, 64, 384), jnp.bfloat16),
            pltpu.VMEM((PAIR, GRID, 64, 9 * C1), jnp.bfloat16),
            pltpu.VMEM((STEPS, GRID, PAIR, 64, C2), jnp.bfloat16),
            pltpu.VMEM((STEPS, PAIR, C3), jnp.float32),
            pltpu.VMEM((STEPS, PAIR, C3), jnp.float32),
            pltpu.VMEM((OWN, 128), jnp.float32),
            dma((OWN,)),
            dma((STEPS, GRID)),
            dma((STEPS, GRID)),
            dma((STEPS,)),
            dma((2, STEPS, 2)),
            dma((2, STEPS, 2)),
            dma((2, STEPS, 2)),
            dma((2, STEPS, 2)),
            dma((GRID + 2 * SIDE,)),
            dma((3, GRID)),
            dma((1,)),
        ],
        compiler_params=pltpu.CompilerParams(vmem_limit_bytes=60 * 2**20, collective_id=0, has_side_effects=True),
        name="encode",
    )(order, pixels, embed_w, embed_g, mixing_w, mixing_g, project_w, extra)


def route_kernel(table, own, wide_x, wide_z, out, held_x, held_z, packed, load_sem, send_sem, recv_sem, keep_sem):
    me = Place()
    wide = (wide_x, wide_z)
    held = (held_x, held_z)

    def loads(which):
        copies = [
            pltpu.make_async_copy(own.at[:, :, which], held[which].at[me.line(which)], load_sem.at[which, 0])
        ]
        for by in range(1, SIDE):
            _, other = me.beside(which, by)
            copies.append(
                pltpu.make_async_copy(wide[which].at[other], held[which].at[other], load_sem.at[which, by])
            )
        return copies

    for which in range(2):
        for copy in loads(which):
            copy.start()
    barrier = pltpu.get_barrier_semaphore()
    for which in range(2):
        for by in range(1, SIDE):
            pl.semaphore_signal(barrier, inc=1, device_id=me.beside(which, by)[0], device_id_type=MESH)
    pl.semaphore_wait(barrier, 2 * (SIDE - 1))

    def target(which, line):
        return out.at[1, :, line] if which else out.at[0, line]

    def send(which, by, incoming):
        device, other = me.beside(1 - which, by)
        line = me.line(1 - which)
        return pltpu.make_async_remote_copy(
            src_ref=packed.at[which, other],
            dst_ref=target(which, other if incoming else line),
            send_sem=send_sem.at[which, by],
            recv_sem=recv_sem.at[which, other if incoming else line],
            device_id=device,
            device_id_type=MESH,
        )

    def keep(which):
        line = me.line(1 - which)
        return pltpu.make_async_copy(packed.at[which, line], target(which, line), keep_sem.at[which])

    def pack(which, other):
        def one(i, carry):
            s, p = i // GRID, lax.rem(i, GRID)
            m = table[(which * SIDE + other) * SIDE * GRID + i]
            packed[which, other, s, p] = held[which][s, m, p]
            return carry

        lax.fori_loop(0, SIDE * GRID, one, 0)

    for by in (2, 1, 3, 0):
        for which in range(2):
            if by == 2:
                for copy in loads(which):
                    copy.wait()
            _, other = me.beside(1 - which, by)
            pack(which, other)
            if by:
                send(which, by, False).start()
            else:
                keep(which).start()
    for which in range(2):
        keep(which).wait()
        for by in range(1, SIDE):
            send(which, by, True).wait_recv()
            send(which, by, False).wait_send()


def route_call(table, own, wide_x, wide_z):
    anywhere = pl.BlockSpec(memory_space=pl.ANY)
    dma = pltpu.SemaphoreType.DMA
    return pl.pallas_call(
        route_kernel,
        in_specs=[pl.BlockSpec(memory_space=pltpu.SMEM)] + [anywhere] * 3,
        out_specs=anywhere,
        out_shape=jax.ShapeDtypeStruct((2, SIDE, SIDE, GRID, 64, C2), jnp.bfloat16),
        scratch_shapes=[
            pltpu.VMEM((SIDE, STEPS, GRID, 64, C2), jnp.bfloat16),
            pltpu.VMEM((SIDE, STEPS, GRID, 64, C2), jnp.bfloat16),
            pltpu.VMEM((2, SIDE, SIDE, GRID, 64, C2), jnp.bfloat16),
            dma((2, SIDE)),
            dma((2, SIDE)),
            dma((2, SIDE)),
            dma((2,)),
        ],
        compiler_params=pltpu.CompilerParams(vmem_limit_bytes=60 * 2**20, collective_id=1, has_side_effects=True),
        name="route",
    )(table, own, wide_x, wide_z)


def decode_kernel(parity, act, stats, weight, gain, out, rows):
    step = pl.program_id(0)
    group = lax.broadcasted_iota(jnp.int32, (128, C3), 1) // 16
    lane = lax.broadcasted_iota(jnp.int32, (128, C3), 0)
    st = stats[...]
    mean = jnp.dot(st, (lane == group).astype(jnp.float32), precision=HI, preferred_element_type=jnp.float32)
    scale = jnp.dot(st, (lane == group + 32).astype(jnp.float32), precision=HI, preferred_element_type=jnp.float32)
    scale = scale * gain[...]
    taken = jnp.broadcast_to(st[:, 64:65], mean.shape) > 0.5
    for i in range(8):
        first = parity[step * 8 + i]
        rows[2 * i] = act[first, i]
        rows[2 * i + 1] = act[1 - first, i]
    values = jnp.dot(rows[...].reshape(-1, C2), weight[...], preferred_element_type=jnp.float32).reshape(-1, 64, C3)
    values = (values - mean[:, None, :]) * scale[:, None, :]
    out[...] = jnp.where(taken[:, None, :], values, 0.0).astype(jnp.bfloat16)


def decode_call(parity, act, stats, weight, gain):
    return pl.pallas_call(
        decode_kernel,
        grid_spec=pltpu.PrefetchScalarGridSpec(
            num_scalar_prefetch=1,
            grid=(16,),
            in_specs=[
                pl.BlockSpec((2, 8, None, 64, C2), lambda i, s: (0, i % 2, i // 2, 0, 0)),
                pl.BlockSpec((16, 128), lambda i, s: (i, 0)),
                pl.BlockSpec((C2, C3), lambda i, s: (0, 0)),
                pl.BlockSpec((1, C3), lambda i, s: (0, 0)),
            ],
            out_specs=pl.BlockSpec((16, 64, C3), lambda i, s: (i, 0, 0)),
            scratch_shapes=[pltpu.VMEM((16, 64, C2), jnp.bfloat16)],
        ),
        out_shape=jax.ShapeDtypeStruct((256, 64, C3), jnp.bfloat16),
        compiler_params=pltpu.CompilerParams(vmem_limit_bytes=60 * 2**20),
        name="decode",
    )(parity, act, stats, weight, gain)


def on_device(
    pixels, destination, embed_weight, embed_gain, mixing_weight, mixing_gain, project_weight, project_gain
):
    targets = destination[:, 0]
    here = jnp.arange(OWN, dtype=jnp.int32)
    ahead = (targets[None, :] < targets[:, None]) | (
        (targets[None, :] == targets[:, None]) & (here[None, :] < here[:, None])
    )
    sorted_at = jnp.sum(ahead.astype(jnp.int32), axis=1)
    hits = sorted_at[None, :] == here[:, None]
    order = jnp.sum(jnp.where(hits, here[None, :], 0), axis=1)
    in_order = jnp.sum(jnp.where(hits, targets[None, :], 0), axis=1)
    lane = jnp.arange(128)
    extra = jnp.where(lane[None, :] == 64, in_order[:, None].astype(jnp.float32), 0.0)
    own, wide_x, wide_z, stats = encode_call(
        order,
        pixels,
        embed_weight,
        embed_gain.reshape(1, C1),
        mixing_weight.reshape(3, 9 * C1, C2),
        mixing_gain.reshape(1, C2),
        project_weight,
        extra,
    )
    c = lax.axis_index("clip")
    z, x = c // SIDE, c % SIDE
    named = jnp.round(stats[:, :, :, 64]).astype(jnp.int32)
    grid = named.reshape(SIDE, SIDE, GRID, STEPS, PAIR)
    steps = jnp.arange(STEPS)
    lines = jnp.arange(SIDE)
    row = lax.dynamic_index_in_dim(grid, z, 0, keepdims=False)[..., 0]
    column = lax.dynamic_index_in_dim(grid, x, 1, keepdims=False)[..., 1]
    to_z = jnp.sum(jnp.where(row[None] == (lines * SIDE + x)[:, None, None, None], steps, 0), axis=-1)
    to_x = jnp.sum(jnp.where(column[None] == (z * SIDE + lines)[:, None, None, None], steps, 0), axis=-1)
    table = jnp.concatenate([to_z.reshape(-1), to_x.reshape(-1)])
    arrived = route_call(table, own, wide_x, wide_z)
    named = named.transpose(1, 0, 2)
    again = jnp.concatenate([jnp.zeros((GRID, 16, 1), bool), named[:, :, 1:] == named[:, :, :-1]], axis=2)
    mine = named == c
    match = jnp.stack([mine & ~again, mine & again], axis=2)
    parity = jnp.sum(jnp.where(match[:, :, 0], here % 2, 0), axis=-1).reshape(128)
    chosen = jnp.sum(jnp.where(match[..., None], stats.transpose(1, 0, 2, 3)[:, :, None], 0.0), axis=3)
    chosen = jnp.where(lane == 64, jnp.any(match, axis=3)[..., None].astype(jnp.float32), chosen)
    out = decode_call(
        parity,
        arrived.reshape(2, 16, GRID, 64, C2),
        chosen.reshape(256, 128),
        project_weight,
        project_gain.reshape(1, C3),
    )
    return out.reshape(256, 8, GRID, C3)


def solution(mesh):
    return jax.shard_map(
        on_device,
        mesh=mesh,
        in_specs=(P(("clip", "patch"), None, None, None), P(("clip", "patch"), None), P(), P(), P(), P(), P(), P()),
        out_specs=P("clip", None, "patch", None),
        check_vma=False,
    )
```

```python
import functools

import jax
import jax.numpy as jnp
from jax import lax
from jax.experimental import pallas as pl
from jax.experimental.pallas import tpu as pltpu
from jax.sharding import PartitionSpec as P

GRID = 8
CAP = 2
OWN = 8
C1, C2, C3 = 128, 256, 512
GROUPS = 32
PAIR = 2
SIDE = 4
STEPS = OWN // PAIR
HI = lax.Precision.HIGHEST
MESH = pl.DeviceIdType.MESH


def fold(rows, size):
    lanes = rows.shape[1]
    lane = lax.broadcasted_iota(jnp.int32, rows.shape, 1)
    step = 1
    while step < size:
        up = pltpu.roll(rows, lanes - step, 1)
        down = pltpu.roll(rows, step, 1)
        rows = rows + jnp.where((lane & step) == 0, up, down)
        step *= 2
    return rows


def group_sums(parts):
    channels = parts[0].shape[1]
    size = channels // GROUPS
    rows = []
    for part in parts:
        total = jnp.sum(part, axis=0, keepdims=True)
        rows += [total[:, i : i + 128] for i in range(0, channels, 128)]
    folded = fold(jnp.concatenate(rows, axis=0), size)
    each = channels // 128
    return [
        jnp.concatenate([folded[n * each + i : n * each + i + 1] for i in range(each)], axis=1)
        for n in range(len(parts))
    ]


def moments(parts):
    rows, channels = parts[0].shape
    inverse = 1.0 / (rows * (channels // GROUPS))
    means = [s * inverse for s in group_sums(parts)]
    squares = []
    for part, mean in zip(parts, means):
        centred = part - mean
        squares.append(centred * centred)
    scales = [lax.rsqrt(s * inverse + 1e-05) for s in group_sums(squares)]
    return means, scales


def silu(v):
    h = 0.5 * v
    return h + h * jnp.tanh(h)


def encode_pair(tubes, embed_w, embed_g, mixing_w, mixing_g, project_w, spread, act, after):
    first = [jnp.dot(t, embed_w[...], preferred_element_type=jnp.float32) for t in tubes]
    means, scales = moments(first)
    for n in range(PAIR):
        wide = silu((first[n] - means[n]) * (scales[n] * embed_g[...]))
        wide = wide.reshape(8, 2, GRID, GRID, C1)
        even, odd = wide[:, 0], wide[:, 1]
        place = lax.broadcasted_iota(jnp.int32, (8 * GRID * GRID, C1), 0) % GRID
        for j in range(3):
            for a, source in ((1, even), (2, odd)):
                flat = source.reshape(8 * GRID * GRID, C1)
                moved = source
                if j == 0:
                    moved = jnp.where(place == 0, 0.0, pltpu.roll(flat, 1, 0))
                elif j == 2:
                    moved = jnp.where(place == GRID - 1, 0.0, pltpu.roll(flat, 8 * GRID * GRID - 1, 0))
                moved = moved.reshape(8, GRID, GRID, C1)
                low = (j * 3 + a) * C1
                for y in range(GRID):
                    block = moved[:, y].reshape(64, C1)
                    spread[n, y, :, low : low + C1] = block.astype(jnp.bfloat16)
                    if a == 2:
                        prior = jnp.concatenate([jnp.zeros((GRID, C1), jnp.float32), block[:-GRID]], axis=0)
                        spread[n, y, :, low - 2 * C1 : low - C1] = prior.astype(jnp.bfloat16)
    second = []
    for n in range(PAIR):
        mid = jnp.dot(spread[n].reshape(512, 9 * C1), mixing_w[1], preferred_element_type=jnp.float32)
        low = jnp.dot(spread[n, 0:7].reshape(448, 9 * C1), mixing_w[0], preferred_element_type=jnp.float32)
        high = jnp.dot(spread[n, 1:8].reshape(448, 9 * C1), mixing_w[2], preferred_element_type=jnp.float32)
        none = jnp.zeros((64, C2), jnp.float32)
        second.append(
            mid + jnp.concatenate([none, low], axis=0) + jnp.concatenate([high, none], axis=0)
        )
    means, scales = moments(second)
    acts = []
    for n in range(PAIR):
        acts.append(silu((second[n] - means[n]) * (scales[n] * mixing_g[...])).astype(jnp.bfloat16))
        act[:, n] = acts[n].reshape(GRID, 64, C2)
    after()
    return moments([jnp.dot(a, project_w[...], preferred_element_type=jnp.float32) for a in acts])


def pick_lanes(mean, scale):
    channel = lax.broadcasted_iota(jnp.int32, (C3, 128), 0)
    lane = lax.broadcasted_iota(jnp.int32, (C3, 128), 1)
    of_mean = ((channel == lane * 16) & (lane < 32)).astype(jnp.float32)
    of_scale = ((channel == (lane - 32) * 16) & (lane >= 32) & (lane < 64)).astype(jnp.float32)
    return jnp.dot(mean, of_mean, precision=HI, preferred_element_type=jnp.float32) + jnp.dot(
        scale, of_scale, precision=HI, preferred_element_type=jnp.float32
    )


class Place:
    def __init__(self):
        self.c, self.p = lax.axis_index("clip"), lax.axis_index("patch")
        self.z, self.x = self.c // SIDE, lax.rem(self.c, SIDE)

    def line(self, which):
        return self.z if which else self.x

    def beside(self, which, by):
        other = lax.rem(self.line(which) + by, SIDE)
        return (other * SIDE + self.x if which else self.z * SIDE + other, self.p), other

    def partner(self, by):
        other = lax.rem(self.p + by, GRID)
        return (self.c, other), other


def exchange_kernel(
    dest, pixels, embed_w, embed_g, mixing_w, mixing_g, project_w,
    arrived, marks, parity, names,
    tubes, spread, act, own, wide_x, wide_z, packed, mean_s, scale_s, tile, tiles, lines, pack_s, name_row, name_s, order,
    pix_sem, send_n, recv_n, keep_n, send_y, recv_y, keep_y, send_g, recv_g, keep_g, send_f, recv_f, send_s, recv_s, keep_s,
    send_l, recv_l, keep_l, send_r, recv_r, keep_r, send_q, recv_q, keep_q,
):
    me = Place()
    wide = (wide_x, wide_z)
    loads = [pltpu.make_async_copy(pixels.at[n], tubes.at[n], pix_sem.at[n]) for n in range(OWN)]
    for load in loads:
        load.start()
    barrier = pltpu.get_barrier_semaphore()
    for by in range(1, GRID):
        pl.semaphore_signal(barrier, inc=1, device_id=me.partner(by)[0], device_id_type=MESH)
    for which in range(2):
        for by in range(1, SIDE):
            pl.semaphore_signal(barrier, inc=1, device_id=me.beside(which, by)[0], device_id_type=MESH)

    d = [dest[k, 0] for k in range(OWN)]
    at = []
    for k in range(OWN):
        ahead = [((d[j] <= d[k]) if j < k else (d[j] < d[k])).astype(jnp.int32) for j in range(OWN) if j != k]
        at.append(functools.reduce(lambda a, b: a + b, ahead))
    lane = lax.broadcasted_iota(jnp.int32, (1, 128), 1)
    row = jnp.zeros((1, 128), jnp.int32)
    for s in range(OWN):
        hit = [(at[k] == s).astype(jnp.int32) for k in range(OWN)]
        order[s] = functools.reduce(lambda a, b: a + b, [hit[k] * k for k in range(OWN)])
        name = functools.reduce(lambda a, b: a + b, [hit[k] * d[k] for k in range(OWN)])
        row = jnp.where(lane == s, name, row)
    name_row[...] = row
    pl.semaphore_wait(barrier, GRID - 1 + 2 * (SIDE - 1))

    def remote(src, dst, send, recv, device):
        return pltpu.make_async_remote_copy(
            src_ref=src, dst_ref=dst, send_sem=send, recv_sem=recv, device_id=device, device_id_type=MESH
        )

    def name_y(by, incoming):
        device, other = me.partner(by)
        to = other if incoming else me.p
        return remote(name_row, names.at[me.c, to], send_n.at[0, by], recv_n.at[0, to], device)

    def name_x(by, incoming):
        device, other = me.beside(0, by)
        to = other if incoming else me.x
        return remote(names.at[me.c], names.at[me.z * SIDE + to], send_n.at[1, by], recv_n.at[1, to], device)

    def name_z(by, incoming):
        device, other = me.beside(1, by)
        to = other if incoming else me.z
        mine = names.at[pl.ds(me.z * SIDE, SIDE)]
        return remote(mine, names.at[pl.ds(to * SIDE, SIDE)], send_n.at[2, by], recv_n.at[2, to], device)

    keep_name = pltpu.make_async_copy(name_row, names.at[me.c, me.p], keep_n.at[0])
    keep_name.start()
    for by in range(1, GRID):
        name_y(by, False).start()
    for load in loads:
        load.wait()

    def across(m, by):
        device, other = me.partner(by)
        return remote(act.at[m, other], own.at[m, me.p], send_y.at[m, by], recv_y.at[m, me.p], device)

    def across_in(m, by):
        device, other = me.partner(by)
        return remote(act.at[m, other], own.at[m, other], send_y.at[m, by], recv_y.at[m, other], device)

    def kept(m):
        return pltpu.make_async_copy(act.at[m, me.p], own.at[m, me.p], keep_y.at[m])

    def stay(which, m):
        return pltpu.make_async_copy(own.at[m, :, which], wide[which].at[me.line(which), m], keep_g.at[which, m])

    def gather(which, m, way):
        device, _ = me.beside(which, 1 if way == 0 else SIDE - 1)
        return remote(
            own.at[m, :, which], wide[which].at[me.line(which), m], send_g.at[which, m, way], recv_g.at[which, m, way], device
        )

    def gather_in(which, m, way):
        device, other = me.beside(which, SIDE - 1 if way == 0 else 1)
        return remote(
            own.at[m, :, which], wide[which].at[other, m], send_g.at[which, m, way], recv_g.at[which, m, way], device
        )

    def half(which, line, m, way):
        return wide[which].at[line, m, pl.ds(way * 4, 4)]

    def pass_on(which, m, way):
        _, origin = me.beside(which, SIDE - 1 if way == 0 else 1)
        device, _ = me.beside(which, 1 if way == 0 else SIDE - 1)
        part = half(which, origin, m, way)
        return remote(part, part, send_f.at[which, m, way], recv_f.at[which, m, way], device)

    def pass_on_in(which, m, way):
        device, origin = me.beside(which, 2)
        part = half(which, origin, m, way)
        return remote(part, part, send_f.at[which, m, way], recv_f.at[which, m, way], device)

    both = [(which, way) for which in range(2) for way in range(2)]

    def start_across(m):
        for by in range(1, GRID):
            across(m, by).start()
        kept(m).start()

    def start_gather(m):
        kept(m).wait()
        for by in range(1, GRID):
            across_in(m, by).wait_recv()
        for which, way in both:
            gather(which, m, way).start()
        for which in range(2):
            stay(which, m).start()

    def start_pass(m):
        for which, way in both:
            gather_in(which, m, way).wait_recv()
            pass_on(which, m, way).start()

    def encode(m):
        def after():
            start_across(m)

            @pl.when(m == 0)
            def _():
                keep_name.wait()
                for by in range(1, GRID):
                    name_y(by, True).wait_recv()
                for by in range(1, SIDE):
                    name_x(by, False).start()

            @pl.when(m >= 1)
            def _():
                start_gather(m - 1)

            @pl.when(m == 1)
            def _():
                for by in range(1, SIDE):
                    name_x(by, True).wait_recv()
                for by in range(1, SIDE):
                    name_z(by, False).start()

            @pl.when(m >= 2)
            def _():
                start_pass(m - 2)

        values = [tubes[order[PAIR * m + n]].reshape(1024, 384) for n in range(PAIR)]
        means, scales = encode_pair(
            values, embed_w, embed_g, mixing_w, mixing_g, project_w, spread, act.at[m], after
        )
        for n in range(PAIR):
            mean_s[m, n : n + 1] = means[n]
            scale_s[m, n : n + 1] = scales[n]

    def loop(m, carry):
        encode(m)
        return carry

    lax.fori_loop(0, STEPS, loop, 0)

    def stat_y(by, incoming):
        device, other = me.partner(by)
        to = other if incoming else me.p
        return remote(tile, tiles.at[to], send_s.at[by], recv_s.at[to], device)

    def stat_line(which, by, incoming):
        device, other = me.beside(which, by)
        to = other if incoming else me.line(which)
        return remote(tiles, lines.at[which, to], send_l.at[which, by], recv_l.at[which, to], device)

    mean = mean_s[...].reshape(OWN, C3)
    scale = scale_s[...].reshape(OWN, C3)
    tile[...] = pick_lanes(mean, scale)
    for by in range(1, GRID):
        stat_y(by, False).start()
    keep_tile = pltpu.make_async_copy(tile, tiles.at[me.p], keep_s.at[0])
    keep_tile.start()
    start_gather(STEPS - 1)
    start_pass(STEPS - 2)
    keep_tile.wait()
    for by in range(1, GRID):
        stat_y(by, True).wait_recv()
    for which in range(2):
        for by in range(1, SIDE):
            stat_line(which, by, False).start()
        pltpu.make_async_copy(tiles, lines.at[which, me.line(which)], keep_l.at[which]).start()
    start_pass(STEPS - 1)
    for by in range(1, SIDE):
        name_z(by, True).wait_recv()
    fetch = pltpu.make_async_copy(names, name_s, keep_n.at[1])
    fetch.start()
    fetch.wait()
    for m in range(STEPS):
        for which, way in both:
            pass_on_in(which, m, way).wait_recv()
        for which in range(2):
            stay(which, m).wait()

    def target(which, line):
        return arrived.at[1, :, line] if which else arrived.at[0, line]

    def mark(which, line):
        return marks.at[1, :, line] if which else marks.at[0, line]

    def route(which, by, incoming):
        device, other = me.beside(1 - which, by)
        to = other if incoming else me.line(1 - which)
        return remote(
            packed.at[which, other], target(which, to), send_r.at[which, by], recv_r.at[which, to], device
        )

    def route_mark(which, by, incoming):
        device, other = me.beside(1 - which, by)
        to = other if incoming else me.line(1 - which)
        return remote(
            pack_s.at[which, other], mark(which, to), send_q.at[which, by], recv_q.at[which, to], device
        )

    def stay_route(which):
        line = me.line(1 - which)
        return pltpu.make_async_copy(packed.at[which, line], target(which, line), keep_r.at[which])

    def stay_mark(which):
        line = me.line(1 - which)
        return pltpu.make_async_copy(pack_s.at[which, line], mark(which, line), keep_q.at[which])

    def find(which, other, s, p):
        owner = s * SIDE + me.x if which else me.z * SIDE + s
        wanted = me.z * SIDE + other if which else other * SIDE + me.x
        m, some = jnp.int32(0), jnp.int32(0)
        for k in range(STEPS):
            hit = name_s[owner, p, 0, PAIR * k + which] == wanted
            m, some = jnp.where(hit, k, m), jnp.where(hit, 1, some)
        return m, some

    def pack(which, other):
        def one(s, carry):
            for p in range(GRID):
                m, _ = find(which, other, s, p)
                packed[which, other, s, p] = wide[which][s, m, p]
            return carry

        lax.fori_loop(0, SIDE, one, 0)

    def pack_mark(which, other):
        def one(s, carry):
            for p in range(GRID):
                m, some = find(which, other, s, p)
                line = lines[which, s, p, pl.ds(PAIR * m + which, 1), :]
                pack_s[which, other, s, p : p + 1, :] = jnp.where(lane == 64, some.astype(jnp.float32), line)
            return carry

        lax.fori_loop(0, SIDE, one, 0)

    for by in (2, 1, 3, 0):
        for which in range(2):
            _, other = me.beside(1 - which, by)
            pack(which, other)
            if by:
                route(which, by, False).start()
            else:
                stay_route(which).start()
    for which in range(2):
        pltpu.make_async_copy(tiles, lines.at[which, me.line(which)], keep_l.at[which]).wait()
        for by in range(1, SIDE):
            stat_line(which, by, True).wait_recv()
    for by in (2, 1, 3, 0):
        for which in range(2):
            _, other = me.beside(1 - which, by)
            pack_mark(which, other)
            if by:
                route_mark(which, by, False).start()
            else:
                stay_mark(which).start()

    def count(i, carry):
        c, p = lax.rem(i, SIDE * SIDE), i // (SIDE * SIDE)
        before = jnp.int32(0)
        for k in range(OWN):
            before = before + (name_s[c, p, 0, k] < me.c).astype(jnp.int32)
        parity[i] = before % 2
        return carry

    lax.fori_loop(0, GRID * SIDE * SIDE, count, 0)

    def drain(m, carry):
        for by in range(1, GRID):
            across(m, by).wait_send()
        for which, way in both:
            gather(which, m, way).wait_send()
            pass_on(which, m, way).wait_send()
        return carry

    lax.fori_loop(0, STEPS, drain, 0)
    for by in range(1, GRID):
        name_y(by, False).wait_send()
        stat_y(by, False).wait_send()
    for by in range(1, SIDE):
        name_x(by, False).wait_send()
        name_z(by, False).wait_send()
        for which in range(2):
            stat_line(which, by, False).wait_send()
    for which in range(2):
        stay_route(which).wait()
        stay_mark(which).wait()
        for by in range(1, SIDE):
            route(which, by, True).wait_recv()
            route(which, by, False).wait_send()
            route_mark(which, by, True).wait_recv()
            route_mark(which, by, False).wait_send()


def exchange_call(dest, pixels, embed_w, embed_g, mixing_w, mixing_g, project_w):
    anywhere = pl.BlockSpec(memory_space=pl.ANY)
    inside = pl.BlockSpec(memory_space=pltpu.VMEM)
    scalar = pl.BlockSpec(memory_space=pltpu.SMEM)
    dma = pltpu.SemaphoreType.DMA
    wide = pltpu.VMEM((SIDE, STEPS, GRID, 64, C2), jnp.bfloat16)
    return pl.pallas_call(
        exchange_kernel,
        in_specs=[scalar, anywhere] + [inside] * 5,
        out_specs=[anywhere, anywhere, scalar, anywhere],
        out_shape=[
            jax.ShapeDtypeStruct((2, SIDE, SIDE, GRID, 64, C2), jnp.bfloat16),
            jax.ShapeDtypeStruct((2, SIDE, SIDE, GRID, 128), jnp.float32),
            jax.ShapeDtypeStruct((128,), jnp.int32),
            jax.ShapeDtypeStruct((SIDE * SIDE, GRID, 1, 128), jnp.int32),
        ],
        scratch_shapes=[
            pltpu.VMEM((OWN, 16, 64, 384), jnp.bfloat16),
            pltpu.VMEM((PAIR, GRID, 64, 9 * C1), jnp.bfloat16),
            pltpu.VMEM((STEPS, GRID, PAIR, 64, C2), jnp.bfloat16),
            pltpu.VMEM((STEPS, GRID, PAIR, 64, C2), jnp.bfloat16),
            wide,
            wide,
            pltpu.VMEM((2, SIDE, SIDE, GRID, 64, C2), jnp.bfloat16),
            pltpu.VMEM((STEPS, PAIR, C3), jnp.float32),
            pltpu.VMEM((STEPS, PAIR, C3), jnp.float32),
            pltpu.VMEM((OWN, 128), jnp.float32),
            pltpu.VMEM((GRID, OWN, 128), jnp.float32),
            pltpu.VMEM((2, SIDE, GRID, OWN, 128), jnp.float32),
            pltpu.VMEM((2, SIDE, SIDE, GRID, 128), jnp.float32),
            pltpu.VMEM((1, 128), jnp.int32),
            pltpu.SMEM((SIDE * SIDE, GRID, 1, 128), jnp.int32),
            pltpu.SMEM((OWN,), jnp.int32),
            dma((OWN,)),
            dma((3, GRID)),
            dma((3, GRID)),
            dma((2,)),
            dma((STEPS, GRID)),
            dma((STEPS, GRID)),
            dma((STEPS,)),
            dma((2, STEPS, 2)),
            dma((2, STEPS, 2)),
            dma((2, STEPS)),
            dma((2, STEPS, 2)),
            dma((2, STEPS, 2)),
            dma((GRID,)),
            dma((GRID,)),
            dma((1,)),
            dma((2, SIDE)),
            dma((2, SIDE)),
            dma((2,)),
            dma((2, SIDE)),
            dma((2, SIDE)),
            dma((2,)),
            dma((2, SIDE)),
            dma((2, SIDE)),
            dma((2,)),
        ],
        compiler_params=pltpu.CompilerParams(vmem_limit_bytes=60 * 2**20, collective_id=0, has_side_effects=True),
        name="exchange",
    )(dest, pixels, embed_w, embed_g, mixing_w, mixing_g, project_w)


def spread_groups(st, base):
    lane = lax.broadcasted_iota(jnp.int32, st.shape, 1)
    return jnp.concatenate(
        [jnp.take_along_axis(st, base + 8 * i + lane // 16, axis=1) for i in range(C3 // 128)], axis=1
    )


def decode_kernel(parity, act, marks, weight, gain, out, rows, st):
    step = pl.program_id(0)
    for i in range(8):
        first = parity[step * 8 + i]
        p = step // 2
        for r in range(CAP):
            which = first if r == 0 else 1 - first
            rows[2 * i + r] = act[which, i]
            st[2 * i + r : 2 * i + r + 1, :] = marks[which, i, pl.ds(p, 1), :]
    mean = spread_groups(st[...], 0)
    scale = spread_groups(st[...], 32) * gain[...]
    taken = jnp.broadcast_to(st[:, 64:65], (16, C3)) > 0.5
    for i in range(0, 16, 4):
        values = jnp.dot(rows[i : i + 4].reshape(-1, C2), weight[...], preferred_element_type=jnp.float32)
        for j in range(4):
            n = i + j
            one = (values[64 * j : 64 * j + 64] - mean[n : n + 1]) * scale[n : n + 1]
            out[n] = jnp.where(taken[n : n + 1], one, 0.0).astype(jnp.bfloat16)


def decode_call(parity, act, marks, weight, gain):
    return pl.pallas_call(
        decode_kernel,
        grid_spec=pltpu.PrefetchScalarGridSpec(
            num_scalar_prefetch=1,
            grid=(16,),
            in_specs=[
                pl.BlockSpec((2, 8, None, 64, C2), lambda i, s: (0, i % 2, i // 2, 0, 0)),
                pl.BlockSpec((2, 8, GRID, 128), lambda i, s: (0, i % 2, 0, 0)),
                pl.BlockSpec((C2, C3), lambda i, s: (0, 0)),
                pl.BlockSpec((1, C3), lambda i, s: (0, 0)),
            ],
            out_specs=pl.BlockSpec((16, 64, C3), lambda i, s: (i, 0, 0)),
            scratch_shapes=[pltpu.VMEM((16, 64, C2), jnp.bfloat16), pltpu.VMEM((16, 128), jnp.float32)],
        ),
        out_shape=jax.ShapeDtypeStruct((256, 64, C3), jnp.bfloat16),
        compiler_params=pltpu.CompilerParams(vmem_limit_bytes=60 * 2**20),
        name="decode",
    )(parity, act, marks, weight, gain)


def on_device(
    pixels, destination, embed_weight, embed_gain, mixing_weight, mixing_gain, project_weight, project_gain
):
    arrived, marks, parity, _ = exchange_call(
        destination,
        pixels,
        embed_weight,
        embed_gain.reshape(1, C1),
        mixing_weight.reshape(3, 9 * C1, C2),
        mixing_gain.reshape(1, C2),
        project_weight,
    )
    out = decode_call(
        parity,
        arrived.reshape(2, 16, GRID, 64, C2),
        marks.reshape(2, 16, GRID, 128),
        project_weight,
        project_gain.reshape(1, C3),
    )
    return out.reshape(256, 8, GRID, C3)


def solution(mesh):
    return jax.shard_map(
        on_device,
        mesh=mesh,
        in_specs=(P(("clip", "patch"), None, None, None), P(("clip", "patch"), None), P(), P(), P(), P(), P(), P()),
        out_specs=P("clip", None, "patch", None),
        check_vma=False,
    )
```

```python
import functools

import jax
import jax.numpy as jnp
from jax import lax
from jax.experimental import pallas as pl
from jax.experimental.pallas import tpu as pltpu
from jax.sharding import PartitionSpec as P

GRID = 8
CAP = 2
OWN = 8
C1, C2, C3 = 128, 256, 512
GROUPS = 32
PAIR = 2
SIDE = 4
STEPS = OWN // PAIR
HI = lax.Precision.HIGHEST
MESH = pl.DeviceIdType.MESH


def fold(rows, size):
    lanes = rows.shape[1]
    lane = lax.broadcasted_iota(jnp.int32, rows.shape, 1)
    step = 1
    while step < size:
        up = pltpu.roll(rows, lanes - step, 1)
        down = pltpu.roll(rows, step, 1)
        rows = rows + jnp.where((lane & step) == 0, up, down)
        step *= 2
    return rows


def group_sums(parts):
    channels = parts[0].shape[1]
    size = channels // GROUPS
    rows = []
    for part in parts:
        total = jnp.sum(part, axis=0, keepdims=True)
        rows += [total[:, i : i + 128] for i in range(0, channels, 128)]
    folded = fold(jnp.concatenate(rows, axis=0), size)
    each = channels // 128
    return [
        jnp.concatenate([folded[n * each + i : n * each + i + 1] for i in range(each)], axis=1)
        for n in range(len(parts))
    ]


def moments(parts):
    rows, channels = parts[0].shape
    inverse = 1.0 / (rows * (channels // GROUPS))
    means = [s * inverse for s in group_sums(parts)]
    squares = []
    for part, mean in zip(parts, means):
        centred = part - mean
        squares.append(centred * centred)
    scales = [lax.rsqrt(s * inverse + 1e-05) for s in group_sums(squares)]
    return means, scales


def silu(v):
    h = 0.5 * v
    return h + h * jnp.tanh(h)


def encode_pair(tubes, embed_w, embed_g, mixing_w, mixing_g, project_w, spread, act, after):
    first = [jnp.dot(t, embed_w[...], preferred_element_type=jnp.float32) for t in tubes]
    means, scales = moments(first)
    for n in range(PAIR):
        wide = silu((first[n] - means[n]) * (scales[n] * embed_g[...]))
        wide = wide.reshape(8, 2, GRID, GRID, C1)
        even, odd = wide[:, 0], wide[:, 1]
        place = lax.broadcasted_iota(jnp.int32, (8 * GRID * GRID, C1), 0) % GRID
        for j in range(3):
            for a, source in ((1, even), (2, odd)):
                flat = source.reshape(8 * GRID * GRID, C1)
                moved = source
                if j == 0:
                    moved = jnp.where(place == 0, 0.0, pltpu.roll(flat, 1, 0))
                elif j == 2:
                    moved = jnp.where(place == GRID - 1, 0.0, pltpu.roll(flat, 8 * GRID * GRID - 1, 0))
                moved = moved.reshape(8, GRID, GRID, C1)
                low = (j * 3 + a) * C1
                for y in range(GRID):
                    block = moved[:, y].reshape(64, C1)
                    spread[n, y, :, low : low + C1] = block.astype(jnp.bfloat16)
                    if a == 2:
                        prior = jnp.concatenate([jnp.zeros((GRID, C1), jnp.float32), block[:-GRID]], axis=0)
                        spread[n, y, :, low - 2 * C1 : low - C1] = prior.astype(jnp.bfloat16)
    second = []
    for n in range(PAIR):
        mid = jnp.dot(spread[n].reshape(512, 9 * C1), mixing_w[1], preferred_element_type=jnp.float32)
        low = jnp.dot(spread[n, 0:7].reshape(448, 9 * C1), mixing_w[0], preferred_element_type=jnp.float32)
        high = jnp.dot(spread[n, 1:8].reshape(448, 9 * C1), mixing_w[2], preferred_element_type=jnp.float32)
        none = jnp.zeros((64, C2), jnp.float32)
        second.append(
            mid + jnp.concatenate([none, low], axis=0) + jnp.concatenate([high, none], axis=0)
        )
    means, scales = moments(second)
    acts = []
    for n in range(PAIR):
        acts.append(silu((second[n] - means[n]) * (scales[n] * mixing_g[...])).astype(jnp.bfloat16))
        act[:, n] = acts[n].reshape(GRID, 64, C2)
    after()
    return moments([jnp.dot(a, project_w[...], preferred_element_type=jnp.float32) for a in acts])


def pick_lanes(mean, scale):
    channel = lax.broadcasted_iota(jnp.int32, (C3, 128), 0)
    lane = lax.broadcasted_iota(jnp.int32, (C3, 128), 1)
    of_mean = ((channel == lane * 16) & (lane < 32)).astype(jnp.float32)
    of_scale = ((channel == (lane - 32) * 16) & (lane >= 32) & (lane < 64)).astype(jnp.float32)
    return jnp.dot(mean, of_mean, precision=HI, preferred_element_type=jnp.float32) + jnp.dot(
        scale, of_scale, precision=HI, preferred_element_type=jnp.float32
    )


class Place:
    def __init__(self):
        self.c, self.p = lax.axis_index("clip"), lax.axis_index("patch")
        self.z, self.x = self.c // SIDE, lax.rem(self.c, SIDE)

    def line(self, which):
        return self.z if which else self.x

    def beside(self, which, by):
        other = lax.rem(self.line(which) + by, SIDE)
        return (other * SIDE + self.x if which else self.z * SIDE + other, self.p), other

    def partner(self, by):
        other = lax.rem(self.p + by, GRID)
        return (self.c, other), other


def exchange_kernel(
    dest, pixels, embed_w, embed_g, mixing_w, mixing_g, project_w,
    arrived, marks, state, names,
    tubes, spread, act, own, wide_x, wide_z, packed, mean_s, scale_s, tile, tiles, lines, pack_s, name_row, name_s, order,
    pix_sem, send_n, recv_n, keep_n, send_y, recv_y, keep_y, send_g, recv_g, keep_g, send_f, recv_f, send_s, recv_s, keep_s,
    send_l, recv_l, keep_l, send_r, recv_r, keep_r, send_q, recv_q, keep_q,
):
    me = Place()
    wide = (wide_x, wide_z)
    loads = [pltpu.make_async_copy(pixels.at[n], tubes.at[n], pix_sem.at[n]) for n in range(OWN)]
    for load in loads:
        load.start()
    barrier = pltpu.get_barrier_semaphore()
    for by in range(1, GRID):
        pl.semaphore_signal(barrier, inc=1, device_id=me.partner(by)[0], device_id_type=MESH)
    for which in range(2):
        for by in range(1, SIDE):
            pl.semaphore_signal(barrier, inc=1, device_id=me.beside(which, by)[0], device_id_type=MESH)

    d = [dest[0, k] for k in range(OWN)]
    at = []
    for k in range(OWN):
        ahead = [((d[j] <= d[k]) if j < k else (d[j] < d[k])).astype(jnp.int32) for j in range(OWN) if j != k]
        at.append(functools.reduce(lambda a, b: a + b, ahead))
    lane = lax.broadcasted_iota(jnp.int32, (1, 128), 1)
    row = jnp.zeros((1, 128), jnp.int32)
    for s in range(OWN):
        hit = [(at[k] == s).astype(jnp.int32) for k in range(OWN)]
        order[s] = functools.reduce(lambda a, b: a + b, [hit[k] * k for k in range(OWN)])
        name = functools.reduce(lambda a, b: a + b, [hit[k] * d[k] for k in range(OWN)])
        row = jnp.where(lane == s, name, row)
    name_row[...] = row
    pl.semaphore_wait(barrier, GRID - 1 + 2 * (SIDE - 1))

    def remote(src, dst, send, recv, device):
        return pltpu.make_async_remote_copy(
            src_ref=src, dst_ref=dst, send_sem=send, recv_sem=recv, device_id=device, device_id_type=MESH
        )

    def name_y(by, incoming):
        device, other = me.partner(by)
        to = other if incoming else me.p
        return remote(name_row, names.at[me.c, to], send_n.at[0, by], recv_n.at[0, to], device)

    def name_x(by, incoming):
        device, other = me.beside(0, by)
        to = other if incoming else me.x
        return remote(names.at[me.c], names.at[me.z * SIDE + to], send_n.at[1, by], recv_n.at[1, to], device)

    def name_z(by, incoming):
        device, other = me.beside(1, by)
        to = other if incoming else me.z
        mine = names.at[pl.ds(me.z * SIDE, SIDE)]
        return remote(mine, names.at[pl.ds(to * SIDE, SIDE)], send_n.at[2, by], recv_n.at[2, to], device)

    keep_name = pltpu.make_async_copy(name_row, names.at[me.c, me.p], keep_n.at[0])
    keep_name.start()
    for by in range(1, GRID):
        name_y(by, False).start()
    for load in loads:
        load.wait()

    def across(m, by):
        device, other = me.partner(by)
        return remote(act.at[m, other], own.at[m, me.p], send_y.at[m, by], recv_y.at[m, me.p], device)

    def across_in(m, by):
        device, other = me.partner(by)
        return remote(act.at[m, other], own.at[m, other], send_y.at[m, by], recv_y.at[m, other], device)

    def kept(m):
        return pltpu.make_async_copy(act.at[m, me.p], own.at[m, me.p], keep_y.at[m])

    def stay(which, m):
        return pltpu.make_async_copy(own.at[m, :, which], wide[which].at[me.line(which), m], keep_g.at[which, m])

    def gather(which, m, way):
        device, _ = me.beside(which, 1 if way == 0 else SIDE - 1)
        return remote(
            own.at[m, :, which], wide[which].at[me.line(which), m], send_g.at[which, m, way], recv_g.at[which, m, way], device
        )

    def gather_in(which, m, way):
        device, other = me.beside(which, SIDE - 1 if way == 0 else 1)
        return remote(
            own.at[m, :, which], wide[which].at[other, m], send_g.at[which, m, way], recv_g.at[which, m, way], device
        )

    def half(which, line, m, way):
        return wide[which].at[line, m, pl.ds(way * 4, 4)]

    def pass_on(which, m, way):
        _, origin = me.beside(which, SIDE - 1 if way == 0 else 1)
        device, _ = me.beside(which, 1 if way == 0 else SIDE - 1)
        part = half(which, origin, m, way)
        return remote(part, part, send_f.at[which, m, way], recv_f.at[which, m, way], device)

    def pass_on_in(which, m, way):
        device, origin = me.beside(which, 2)
        part = half(which, origin, m, way)
        return remote(part, part, send_f.at[which, m, way], recv_f.at[which, m, way], device)

    both = [(which, way) for which in range(2) for way in range(2)]

    def start_across(m):
        for by in range(1, GRID):
            across(m, by).start()
        kept(m).start()

    def start_gather(m):
        kept(m).wait()
        for by in range(1, GRID):
            across_in(m, by).wait_recv()
        for which, way in both:
            gather(which, m, way).start()
        for which in range(2):
            stay(which, m).start()

    def start_pass(m):
        for which, way in both:
            gather_in(which, m, way).wait_recv()
            pass_on(which, m, way).start()

    def encode(m):
        def after():
            start_across(m)

            @pl.when(m == 0)
            def _():
                keep_name.wait()
                for by in range(1, GRID):
                    name_y(by, True).wait_recv()
                for by in range(1, SIDE):
                    name_x(by, False).start()

            @pl.when(m >= 1)
            def _():
                start_gather(m - 1)

            @pl.when(m == 1)
            def _():
                for by in range(1, SIDE):
                    name_x(by, True).wait_recv()
                for by in range(1, SIDE):
                    name_z(by, False).start()

            @pl.when(m >= 2)
            def _():
                start_pass(m - 2)

        values = [tubes[order[PAIR * m + n]].reshape(1024, 384) for n in range(PAIR)]
        means, scales = encode_pair(
            values, embed_w, embed_g, mixing_w, mixing_g, project_w, spread, act.at[m], after
        )
        for n in range(PAIR):
            mean_s[m, n : n + 1] = means[n]
            scale_s[m, n : n + 1] = scales[n]

    def loop(m, carry):
        encode(m)
        return carry

    lax.fori_loop(0, STEPS, loop, 0)

    def stat_y(by, incoming):
        device, other = me.partner(by)
        to = other if incoming else me.p
        return remote(tile, tiles.at[to], send_s.at[by], recv_s.at[to], device)

    def stat_line(which, by, incoming):
        device, other = me.beside(which, by)
        to = other if incoming else me.line(which)
        return remote(tiles, lines.at[which, to], send_l.at[which, by], recv_l.at[which, to], device)

    mean = mean_s[...].reshape(OWN, C3)
    scale = scale_s[...].reshape(OWN, C3)
    tile[...] = pick_lanes(mean, scale)
    for by in range(1, GRID):
        stat_y(by, False).start()
    keep_tile = pltpu.make_async_copy(tile, tiles.at[me.p], keep_s.at[0])
    keep_tile.start()
    start_gather(STEPS - 1)
    start_pass(STEPS - 2)
    keep_tile.wait()
    for by in range(1, GRID):
        stat_y(by, True).wait_recv()
    for which in range(2):
        for by in range(1, SIDE):
            stat_line(which, by, False).start()
        pltpu.make_async_copy(tiles, lines.at[which, me.line(which)], keep_l.at[which]).start()
    start_pass(STEPS - 1)
    for by in range(1, SIDE):
        name_z(by, True).wait_recv()
    fetch = pltpu.make_async_copy(names, name_s, keep_n.at[1])
    fetch.start()
    fetch.wait()
    for m in range(STEPS):
        for which, way in both:
            pass_on_in(which, m, way).wait_recv()
        for which in range(2):
            stay(which, m).wait()

    def target(which, line):
        return arrived.at[1, :, line] if which else arrived.at[0, line]

    def mark(which, line):
        return marks.at[1, :, line] if which else marks.at[0, line]

    def route(which, by, incoming):
        device, other = me.beside(1 - which, by)
        to = other if incoming else me.line(1 - which)
        return remote(
            packed.at[which, other], target(which, to), send_r.at[which, by], recv_r.at[which, to], device
        )

    def route_mark(which, by, incoming):
        device, other = me.beside(1 - which, by)
        to = other if incoming else me.line(1 - which)
        return remote(
            pack_s.at[which, other], mark(which, to), send_q.at[which, by], recv_q.at[which, to], device
        )

    def stay_route(which):
        line = me.line(1 - which)
        return pltpu.make_async_copy(packed.at[which, line], target(which, line), keep_r.at[which])

    def stay_mark(which):
        line = me.line(1 - which)
        return pltpu.make_async_copy(pack_s.at[which, line], mark(which, line), keep_q.at[which])

    def find(which, other, s, p):
        owner = s * SIDE + me.x if which else me.z * SIDE + s
        wanted = me.z * SIDE + other if which else other * SIDE + me.x
        m = jnp.int32(0)
        for k in range(STEPS):
            m = jnp.where(name_s[owner, p, 0, PAIR * k + which] == wanted, k, m)
        return m

    def pack(which, other):
        def one(s, carry):
            for p in range(GRID):
                m = find(which, other, s, p)
                packed[which, other, s, p] = wide[which][s, m, p]
            return carry

        lax.fori_loop(0, SIDE, one, 0)

    def pack_mark(which, other):
        def one(s, carry):
            for p in range(GRID):
                m = find(which, other, s, p)
                pack_s[which, other, s, p : p + 1, :] = lines[which, s, p, pl.ds(PAIR * m + which, 1), :]
            return carry

        lax.fori_loop(0, SIDE, one, 0)

    for by in (2, 1, 3, 0):
        for which in range(2):
            _, other = me.beside(1 - which, by)
            pack(which, other)
            if by:
                route(which, by, False).start()
            else:
                stay_route(which).start()
    for which in range(2):
        pltpu.make_async_copy(tiles, lines.at[which, me.line(which)], keep_l.at[which]).wait()
        for by in range(1, SIDE):
            stat_line(which, by, True).wait_recv()
    for by in (2, 1, 3, 0):
        for which in range(2):
            _, other = me.beside(1 - which, by)
            pack_mark(which, other)
            if by:
                route_mark(which, by, False).start()
            else:
                stay_mark(which).start()

    def count(i, carry):
        c, p = lax.rem(i, SIDE * SIDE), i // (SIDE * SIDE)
        before, number = jnp.int32(0), jnp.int32(0)
        for k in range(OWN):
            name = name_s[c, p, 0, k]
            before = before + (name < me.c).astype(jnp.int32)
            number = number + (name == me.c).astype(jnp.int32)
        state[i] = before % 2 + 2 * number
        return carry

    lax.fori_loop(0, GRID * SIDE * SIDE, count, 0)

    def drain(m, carry):
        for by in range(1, GRID):
            across(m, by).wait_send()
        for which, way in both:
            gather(which, m, way).wait_send()
            pass_on(which, m, way).wait_send()
        return carry

    lax.fori_loop(0, STEPS, drain, 0)
    for by in range(1, GRID):
        name_y(by, False).wait_send()
        stat_y(by, False).wait_send()
    for by in range(1, SIDE):
        name_x(by, False).wait_send()
        name_z(by, False).wait_send()
        for which in range(2):
            stat_line(which, by, False).wait_send()
    for which in range(2):
        stay_route(which).wait()
        stay_mark(which).wait()
        for by in range(1, SIDE):
            route(which, by, True).wait_recv()
            route(which, by, False).wait_send()
            route_mark(which, by, True).wait_recv()
            route_mark(which, by, False).wait_send()


def exchange_call(dest, pixels, embed_w, embed_g, mixing_w, mixing_g, project_w):
    anywhere = pl.BlockSpec(memory_space=pl.ANY)
    inside = pl.BlockSpec(memory_space=pltpu.VMEM)
    scalar = pl.BlockSpec(memory_space=pltpu.SMEM)
    dma = pltpu.SemaphoreType.DMA
    wide = pltpu.VMEM((SIDE, STEPS, GRID, 64, C2), jnp.bfloat16)
    return pl.pallas_call(
        exchange_kernel,
        in_specs=[scalar, anywhere] + [inside] * 5,
        out_specs=[anywhere, anywhere, scalar, anywhere],
        out_shape=[
            jax.ShapeDtypeStruct((2, SIDE, SIDE, GRID, 64, C2), jnp.bfloat16),
            jax.ShapeDtypeStruct((2, SIDE, SIDE, GRID, 128), jnp.float32),
            jax.ShapeDtypeStruct((128,), jnp.int32),
            jax.ShapeDtypeStruct((SIDE * SIDE, GRID, 1, 128), jnp.int32),
        ],
        scratch_shapes=[
            pltpu.VMEM((OWN, 16, 64, 384), jnp.bfloat16),
            pltpu.VMEM((PAIR, GRID, 64, 9 * C1), jnp.bfloat16),
            pltpu.VMEM((STEPS, GRID, PAIR, 64, C2), jnp.bfloat16),
            pltpu.VMEM((STEPS, GRID, PAIR, 64, C2), jnp.bfloat16),
            wide,
            wide,
            pltpu.VMEM((2, SIDE, SIDE, GRID, 64, C2), jnp.bfloat16),
            pltpu.VMEM((STEPS, PAIR, C3), jnp.float32),
            pltpu.VMEM((STEPS, PAIR, C3), jnp.float32),
            pltpu.VMEM((OWN, 128), jnp.float32),
            pltpu.VMEM((GRID, OWN, 128), jnp.float32),
            pltpu.VMEM((2, SIDE, GRID, OWN, 128), jnp.float32),
            pltpu.VMEM((2, SIDE, SIDE, GRID, 128), jnp.float32),
            pltpu.VMEM((1, 128), jnp.int32),
            pltpu.SMEM((SIDE * SIDE, GRID, 1, 128), jnp.int32),
            pltpu.SMEM((OWN,), jnp.int32),
            dma((OWN,)),
            dma((3, GRID)),
            dma((3, GRID)),
            dma((2,)),
            dma((STEPS, GRID)),
            dma((STEPS, GRID)),
            dma((STEPS,)),
            dma((2, STEPS, 2)),
            dma((2, STEPS, 2)),
            dma((2, STEPS)),
            dma((2, STEPS, 2)),
            dma((2, STEPS, 2)),
            dma((GRID,)),
            dma((GRID,)),
            dma((1,)),
            dma((2, SIDE)),
            dma((2, SIDE)),
            dma((2,)),
            dma((2, SIDE)),
            dma((2, SIDE)),
            dma((2,)),
            dma((2, SIDE)),
            dma((2, SIDE)),
            dma((2,)),
        ],
        compiler_params=pltpu.CompilerParams(vmem_limit_bytes=60 * 2**20, collective_id=0, has_side_effects=True),
        name="exchange",
    )(dest, pixels, embed_w, embed_g, mixing_w, mixing_g, project_w)


def spread_groups(st, base):
    lane = lax.broadcasted_iota(jnp.int32, st.shape, 1)
    return jnp.concatenate(
        [jnp.take_along_axis(st, base + 8 * i + lane // 16, axis=1) for i in range(C3 // 128)], axis=1
    )


PART = 16
PARTS = 256 // PART


def decode_kernel(state, arrived, marks, weight, gain, out, act, ready, rows, st, in_sem, out_sem):
    def fetch(i):
        p, c = i // 2, pl.ds(lax.rem(i, 2) * 8, 8)
        return pltpu.make_async_copy(arrived.at[:, c, p], act.at[i], in_sem.at[i])

    def put(i):
        return pltpu.make_async_copy(ready.at[i], out.at[pl.ds(i * PART, PART)], out_sem.at[i])

    def begin(i, carry):
        fetch(i).start()
        return carry

    lax.fori_loop(0, PARTS, begin, 0)

    def work(i, carry):
        p, c = i // 2, lax.rem(i, 2) * 8
        fetch(i).wait()
        for j in range(8):
            first, number = state[i * 8 + j] % 2, state[i * 8 + j] // 2
            for r in range(CAP):
                which = first if r == 0 else 1 - first
                n = CAP * j + r
                rows[n] = jnp.where(number > r, act[i, which, j], jnp.zeros((64, C2), jnp.bfloat16))
                st[n : n + 1, :] = jnp.where(number > r, marks[which, c + j, pl.ds(p, 1), :], 0.0)
        mean = spread_groups(st[...], 0)
        scale = spread_groups(st[...], 32) * gain[...]
        for k in range(0, PART, 4):
            values = jnp.dot(rows[k : k + 4].reshape(-1, C2), weight[...], preferred_element_type=jnp.float32)
            for j in range(4):
                n = k + j
                one = (values[64 * j : 64 * j + 64] - mean[n : n + 1]) * scale[n : n + 1]
                ready[i, n] = one.astype(jnp.bfloat16)
        put(i).start()
        return carry

    lax.fori_loop(0, PARTS, work, 0)

    def finish(i, carry):
        put(i).wait()
        return carry

    lax.fori_loop(0, PARTS, finish, 0)


def decode_call(state, arrived, marks, weight, gain):
    anywhere = pl.BlockSpec(memory_space=pl.ANY)
    inside = pl.BlockSpec(memory_space=pltpu.VMEM)
    return pl.pallas_call(
        decode_kernel,
        in_specs=[pl.BlockSpec(memory_space=pltpu.SMEM), anywhere, inside, inside, inside],
        out_specs=anywhere,
        scratch_shapes=[
            pltpu.VMEM((PARTS, 2, 8, 64, C2), jnp.bfloat16),
            pltpu.VMEM((PARTS, PART, 64, C3), jnp.bfloat16),
            pltpu.VMEM((PART, 64, C2), jnp.bfloat16),
            pltpu.VMEM((PART, 128), jnp.float32),
            pltpu.SemaphoreType.DMA((PARTS,)),
            pltpu.SemaphoreType.DMA((PARTS,)),
        ],
        out_shape=jax.ShapeDtypeStruct((256, 64, C3), jnp.bfloat16),
        compiler_params=pltpu.CompilerParams(vmem_limit_bytes=60 * 2**20),
        name="decode",
    )(state, arrived, marks, weight, gain)


def on_device(
    pixels, destination, embed_weight, embed_gain, mixing_weight, mixing_gain, project_weight, project_gain
):
    arrived, marks, state, _ = exchange_call(
        destination.reshape(1, OWN),
        pixels,
        embed_weight,
        embed_gain.reshape(1, C1),
        mixing_weight.reshape(3, 9 * C1, C2),
        mixing_gain.reshape(1, C2),
        project_weight,
    )
    out = decode_call(
        state,
        arrived.reshape(2, 16, GRID, 64, C2),
        marks.reshape(2, 16, GRID, 128),
        project_weight,
        project_gain.reshape(1, C3),
    )
    return out.reshape(256, 8, GRID, C3)


def solution(mesh):
    return jax.shard_map(
        on_device,
        mesh=mesh,
        in_specs=(P(("clip", "patch"), None, None, None), P(("clip", "patch"), None), P(), P(), P(), P(), P(), P()),
        out_specs=P("clip", None, "patch", None),
        check_vma=False,
    )
```

```python
import functools

import jax
import jax.numpy as jnp
from jax import lax
from jax.experimental import pallas as pl
from jax.experimental.pallas import tpu as pltpu
from jax.sharding import PartitionSpec as P

GRID = 8
CAP = 2
OWN = 8
C1, C2, C3 = 128, 256, 512
GROUPS = 32
PAIR = 2
SIDE = 4
STEPS = OWN // PAIR
HI = lax.Precision.HIGHEST
MESH = pl.DeviceIdType.MESH


def fold(rows, size):
    lanes = rows.shape[1]
    lane = lax.broadcasted_iota(jnp.int32, rows.shape, 1)
    step = 1
    while step < size:
        up = pltpu.roll(rows, lanes - step, 1)
        down = pltpu.roll(rows, step, 1)
        rows = rows + jnp.where((lane & step) == 0, up, down)
        step *= 2
    return rows


def group_sums(parts):
    channels = parts[0].shape[1]
    size = channels // GROUPS
    rows = []
    for part in parts:
        total = jnp.sum(part, axis=0, keepdims=True)
        rows += [total[:, i : i + 128] for i in range(0, channels, 128)]
    folded = fold(jnp.concatenate(rows, axis=0), size)
    each = channels // 128
    return [
        jnp.concatenate([folded[n * each + i : n * each + i + 1] for i in range(each)], axis=1)
        for n in range(len(parts))
    ]


def moments(parts):
    rows, channels = parts[0].shape
    inverse = 1.0 / (rows * (channels // GROUPS))
    means = [s * inverse for s in group_sums(parts)]
    squares = []
    for part, mean in zip(parts, means):
        centred = part - mean
        squares.append(centred * centred)
    scales = [lax.rsqrt(s * inverse + 1e-05) for s in group_sums(squares)]
    return means, scales


def silu(v):
    h = 0.5 * v
    return h + h * jnp.tanh(h)


def encode_pair(tubes, embed_w, embed_g, mixing_w, mixing_g, project_w, spread, act, after):
    first = [jnp.dot(t, embed_w[...], preferred_element_type=jnp.float32) for t in tubes]
    means, scales = moments(first)
    for n in range(PAIR):
        wide = silu((first[n] - means[n]) * (scales[n] * embed_g[...]))
        wide = wide.reshape(8, 2, GRID, GRID, C1)
        even, odd = wide[:, 0], wide[:, 1]
        place = lax.broadcasted_iota(jnp.int32, (8 * GRID * GRID, C1), 0) % GRID
        for j in range(3):
            for a, source in ((1, even), (2, odd)):
                flat = source.reshape(8 * GRID * GRID, C1)
                moved = source
                if j == 0:
                    moved = jnp.where(place == 0, 0.0, pltpu.roll(flat, 1, 0))
                elif j == 2:
                    moved = jnp.where(place == GRID - 1, 0.0, pltpu.roll(flat, 8 * GRID * GRID - 1, 0))
                moved = moved.reshape(8, GRID, GRID, C1)
                low = (j * 3 + a) * C1
                for y in range(GRID):
                    block = moved[:, y].reshape(64, C1)
                    spread[n, y, :, low : low + C1] = block.astype(jnp.bfloat16)
                    if a == 2:
                        prior = jnp.concatenate([jnp.zeros((GRID, C1), jnp.float32), block[:-GRID]], axis=0)
                        spread[n, y, :, low - 2 * C1 : low - C1] = prior.astype(jnp.bfloat16)
    second = []
    for n in range(PAIR):
        mid = jnp.dot(spread[n].reshape(512, 9 * C1), mixing_w[1], preferred_element_type=jnp.float32)
        low = jnp.dot(spread[n, 0:7].reshape(448, 9 * C1), mixing_w[0], preferred_element_type=jnp.float32)
        high = jnp.dot(spread[n, 1:8].reshape(448, 9 * C1), mixing_w[2], preferred_element_type=jnp.float32)
        none = jnp.zeros((64, C2), jnp.float32)
        second.append(
            mid + jnp.concatenate([none, low], axis=0) + jnp.concatenate([high, none], axis=0)
        )
    means, scales = moments(second)
    acts = []
    for n in range(PAIR):
        acts.append(silu((second[n] - means[n]) * (scales[n] * mixing_g[...])).astype(jnp.bfloat16))
        act[:, n] = acts[n].reshape(GRID, 64, C2)
    after()
    return moments([jnp.dot(a, project_w[...], preferred_element_type=jnp.float32) for a in acts])


def pick_lanes(mean, scale):
    channel = lax.broadcasted_iota(jnp.int32, (C3, 128), 0)
    lane = lax.broadcasted_iota(jnp.int32, (C3, 128), 1)
    of_mean = ((channel == lane * 16) & (lane < 32)).astype(jnp.float32)
    of_scale = ((channel == (lane - 32) * 16) & (lane >= 32) & (lane < 64)).astype(jnp.float32)
    return jnp.dot(mean, of_mean, precision=HI, preferred_element_type=jnp.float32) + jnp.dot(
        scale, of_scale, precision=HI, preferred_element_type=jnp.float32
    )


class Place:
    def __init__(self):
        self.c, self.p = lax.axis_index("clip"), lax.axis_index("patch")
        self.z, self.x = self.c // SIDE, lax.rem(self.c, SIDE)

    def line(self, which):
        return self.z if which else self.x

    def beside(self, which, by):
        other = lax.rem(self.line(which) + by, SIDE)
        return (other * SIDE + self.x if which else self.z * SIDE + other, self.p), other

    def partner(self, by):
        other = lax.rem(self.p + by, GRID)
        return (self.c, other), other


def exchange_kernel(
    dest, pixels, embed_w, embed_g, mixing_w, mixing_g, project_w,
    arrived, marks, state, names,
    tubes, spread, act, own, near_x, near_z, far_x, far_z, packed, mean_s, scale_s, tile, tiles, lines, pack_s, name_row, name_s, order,
    pix_sem, send_n, recv_n, keep_n, send_y, recv_y, keep_y, send_g, recv_g, send_f, recv_f, send_s, recv_s, keep_s,
    send_l, recv_l, keep_l, send_r, recv_r, keep_r, send_q, recv_q, keep_q,
):
    me = Place()
    near, far = (near_x, near_z), (far_x, far_z)
    loads = [pltpu.make_async_copy(pixels.at[n], tubes.at[n], pix_sem.at[n]) for n in range(OWN)]
    for load in loads:
        load.start()
    barrier = pltpu.get_barrier_semaphore()
    for by in range(1, GRID):
        pl.semaphore_signal(barrier, inc=1, device_id=me.partner(by)[0], device_id_type=MESH)
    for which in range(2):
        for by in range(1, SIDE):
            pl.semaphore_signal(barrier, inc=1, device_id=me.beside(which, by)[0], device_id_type=MESH)

    d = [dest[0, k] for k in range(OWN)]
    at = []
    for k in range(OWN):
        ahead = [((d[j] <= d[k]) if j < k else (d[j] < d[k])).astype(jnp.int32) for j in range(OWN) if j != k]
        at.append(functools.reduce(lambda a, b: a + b, ahead))
    lane = lax.broadcasted_iota(jnp.int32, (1, 128), 1)
    row = jnp.zeros((1, 128), jnp.int32)
    for s in range(OWN):
        hit = [(at[k] == s).astype(jnp.int32) for k in range(OWN)]
        order[s] = functools.reduce(lambda a, b: a + b, [hit[k] * k for k in range(OWN)])
        name = functools.reduce(lambda a, b: a + b, [hit[k] * d[k] for k in range(OWN)])
        row = jnp.where(lane == s, name, row)
    name_row[...] = row
    pl.semaphore_wait(barrier, GRID - 1 + 2 * (SIDE - 1))

    def remote(src, dst, send, recv, device):
        return pltpu.make_async_remote_copy(
            src_ref=src, dst_ref=dst, send_sem=send, recv_sem=recv, device_id=device, device_id_type=MESH
        )

    def name_y(by, incoming):
        device, other = me.partner(by)
        to = other if incoming else me.p
        return remote(name_row, names.at[me.c, to], send_n.at[0, by], recv_n.at[0, to], device)

    def name_x(by, incoming):
        device, other = me.beside(0, by)
        to = other if incoming else me.x
        return remote(names.at[me.c], names.at[me.z * SIDE + to], send_n.at[1, by], recv_n.at[1, to], device)

    def name_z(by, incoming):
        device, other = me.beside(1, by)
        to = other if incoming else me.z
        mine = names.at[pl.ds(me.z * SIDE, SIDE)]
        return remote(mine, names.at[pl.ds(to * SIDE, SIDE)], send_n.at[2, by], recv_n.at[2, to], device)

    keep_name = pltpu.make_async_copy(name_row, names.at[me.c, me.p], keep_n.at[0])
    keep_name.start()
    for by in range(1, GRID):
        name_y(by, False).start()
    for load in loads:
        load.wait()

    def across(m, by):
        device, other = me.partner(by)
        return remote(act.at[m, other], own.at[m, me.p], send_y.at[m, by], recv_y.at[m, me.p], device)

    def across_in(m, by):
        device, other = me.partner(by)
        return remote(act.at[m, other], own.at[m, other], send_y.at[m, by], recv_y.at[m, other], device)

    def kept(m):
        return pltpu.make_async_copy(act.at[m, me.p], own.at[m, me.p], keep_y.at[m])

    def gather(which, m, way):
        device, _ = me.beside(which, 1 if way == 0 else SIDE - 1)
        return remote(
            own.at[m, :, which], near[which].at[way, m], send_g.at[which, m, way], recv_g.at[which, m, way], device
        )

    def pass_on(which, m, way):
        device, _ = me.beside(which, 1 if way == 0 else SIDE - 1)
        part = pl.ds(way * 4, 4)
        return remote(
            near[which].at[way, m, part], far[which].at[m, part], send_f.at[which, m, way], recv_f.at[which, m, way], device
        )

    both = [(which, way) for which in range(2) for way in range(2)]

    def start_across(m):
        for by in range(1, GRID):
            across(m, by).start()
        kept(m).start()

    def start_gather(m):
        kept(m).wait()
        for by in range(1, GRID):
            across_in(m, by).wait_recv()
        for which, way in both:
            gather(which, m, way).start()

    def start_pass(m):
        for which, way in both:
            gather(which, m, way).wait_recv()
            pass_on(which, m, way).start()

    def encode(m):
        def after():
            start_across(m)

            @pl.when(m == 0)
            def _():
                keep_name.wait()
                for by in range(1, GRID):
                    name_y(by, True).wait_recv()
                for by in range(1, SIDE):
                    name_x(by, False).start()

            @pl.when(m >= 1)
            def _():
                start_gather(m - 1)

            @pl.when(m == 1)
            def _():
                for by in range(1, SIDE):
                    name_x(by, True).wait_recv()
                for by in range(1, SIDE):
                    name_z(by, False).start()

            @pl.when(m >= 2)
            def _():
                start_pass(m - 2)

        values = [tubes[order[PAIR * m + n]].reshape(1024, 384) for n in range(PAIR)]
        means, scales = encode_pair(
            values, embed_w, embed_g, mixing_w, mixing_g, project_w, spread, act.at[m], after
        )
        for n in range(PAIR):
            mean_s[m, n : n + 1] = means[n]
            scale_s[m, n : n + 1] = scales[n]

    def loop(m, carry):
        encode(m)
        return carry

    lax.fori_loop(0, STEPS, loop, 0)

    def stat_y(by, incoming):
        device, other = me.partner(by)
        to = other if incoming else me.p
        return remote(tile, tiles.at[to], send_s.at[by], recv_s.at[to], device)

    def stat_line(which, by, incoming):
        device, other = me.beside(which, by)
        to = other if incoming else me.line(which)
        return remote(tiles, lines.at[which, to], send_l.at[which, by], recv_l.at[which, to], device)

    mean = mean_s[...].reshape(OWN, C3)
    scale = scale_s[...].reshape(OWN, C3)
    tile[...] = pick_lanes(mean, scale)
    for by in range(1, GRID):
        stat_y(by, False).start()
    keep_tile = pltpu.make_async_copy(tile, tiles.at[me.p], keep_s.at[0])
    keep_tile.start()
    start_gather(STEPS - 1)
    for by in range(1, SIDE):
        name_z(by, True).wait_recv()
    fetch_names = pltpu.make_async_copy(names, name_s, keep_n.at[1])
    fetch_names.start()
    start_pass(STEPS - 2)
    keep_tile.wait()
    for by in range(1, GRID):
        stat_y(by, True).wait_recv()
    for which in range(2):
        for by in range(1, SIDE):
            stat_line(which, by, False).start()
        pltpu.make_async_copy(tiles, lines.at[which, me.line(which)], keep_l.at[which]).start()
    def target(which, line, s):
        return arrived.at[1, s, line] if which else arrived.at[0, line, s]

    def mark(which, line):
        return marks.at[1, :, line] if which else marks.at[0, line]

    def source(which, kind):
        return lax.rem(me.line(which) + (0, SIDE - 1, 1, 2)[kind], SIDE)

    def route(which, by, kind, incoming):
        device, other = me.beside(1 - which, by)
        to, s = other if incoming else me.line(1 - which), source(which, kind)
        return remote(
            packed.at[which, other, s], target(which, to, s), send_r.at[which, by, kind], recv_r.at[which, to, kind], device
        )

    def route_mark(which, by, incoming):
        device, other = me.beside(1 - which, by)
        to = other if incoming else me.line(1 - which)
        return remote(
            pack_s.at[which, other], mark(which, to), send_q.at[which, by], recv_q.at[which, to], device
        )

    def stay_route(which, kind):
        line, s = me.line(1 - which), source(which, kind)
        return pltpu.make_async_copy(packed.at[which, line, s], target(which, line, s), keep_r.at[which, kind])

    def stay_mark(which):
        line = me.line(1 - which)
        return pltpu.make_async_copy(pack_s.at[which, line], mark(which, line), keep_q.at[which])

    def find(which, other, s, p):
        owner = s * SIDE + me.x if which else me.z * SIDE + s
        wanted = me.z * SIDE + other if which else other * SIDE + me.x
        m = jnp.int32(0)
        for k in range(STEPS):
            m = jnp.where(name_s[owner, p, 0, PAIR * k + which] == wanted, k, m)
        return m

    def pack(which, other, kind):
        s = source(which, kind)

        def one(p, carry):
            m = find(which, other, s, p)
            if kind == 0:
                packed[which, other, s, p] = own[m, p, which]
            elif kind == 3:
                packed[which, other, s, p] = far[which][m, p]
            else:
                packed[which, other, s, p] = near[which][kind - 1, m, p]
            return carry

        lax.fori_loop(0, GRID, one, 0)

    def start_route(kinds, hops):
        for by in hops:
            for which in range(2):
                for kind in kinds:
                    _, other = me.beside(1 - which, by)
                    pack(which, other, kind)
                    if by:
                        route(which, by, kind, False).start()
                    else:
                        stay_route(which, kind).start()

    def pack_mark(which, other):
        def one(s, carry):
            for p in range(GRID):
                m = find(which, other, s, p)
                pack_s[which, other, s, p : p + 1, :] = lines[which, s, p, pl.ds(PAIR * m + which, 1), :]
            return carry

        lax.fori_loop(0, SIDE, one, 0)

    fetch_names.wait()
    start_route((0,), (2, 1, 3))
    start_pass(STEPS - 1)
    start_route((1, 2), (2, 1, 3))
    for m in range(STEPS):
        for which, way in both:
            pass_on(which, m, way).wait_recv()
    start_route((3,), (2, 1, 3))
    start_route((0, 1, 2, 3), (0,))
    for which in range(2):
        pltpu.make_async_copy(tiles, lines.at[which, me.line(which)], keep_l.at[which]).wait()
        for by in range(1, SIDE):
            stat_line(which, by, True).wait_recv()
    for by in (2, 1, 3, 0):
        for which in range(2):
            _, other = me.beside(1 - which, by)
            pack_mark(which, other)
            if by:
                route_mark(which, by, False).start()
            else:
                stay_mark(which).start()

    def count(i, carry):
        c, p = lax.rem(i, SIDE * SIDE), i // (SIDE * SIDE)
        before, number = jnp.int32(0), jnp.int32(0)
        for k in range(OWN):
            name = name_s[c, p, 0, k]
            before = before + (name < me.c).astype(jnp.int32)
            number = number + (name == me.c).astype(jnp.int32)
        state[i] = before % 2 + 2 * number
        return carry

    lax.fori_loop(0, GRID * SIDE * SIDE, count, 0)

    def drain(m, carry):
        for by in range(1, GRID):
            across(m, by).wait_send()
        for which, way in both:
            gather(which, m, way).wait_send()
            pass_on(which, m, way).wait_send()
        return carry

    lax.fori_loop(0, STEPS, drain, 0)
    for by in range(1, GRID):
        name_y(by, False).wait_send()
        stat_y(by, False).wait_send()
    for by in range(1, SIDE):
        name_x(by, False).wait_send()
        name_z(by, False).wait_send()
        for which in range(2):
            stat_line(which, by, False).wait_send()
    for which in range(2):
        stay_mark(which).wait()
        for kind in range(SIDE):
            stay_route(which, kind).wait()
            for by in range(1, SIDE):
                route(which, by, kind, True).wait_recv()
                route(which, by, kind, False).wait_send()
        for by in range(1, SIDE):
            route_mark(which, by, True).wait_recv()
            route_mark(which, by, False).wait_send()


def exchange_call(dest, pixels, embed_w, embed_g, mixing_w, mixing_g, project_w):
    anywhere = pl.BlockSpec(memory_space=pl.ANY)
    inside = pl.BlockSpec(memory_space=pltpu.VMEM)
    scalar = pl.BlockSpec(memory_space=pltpu.SMEM)
    dma = pltpu.SemaphoreType.DMA
    near = pltpu.VMEM((2, STEPS, GRID, 64, C2), jnp.bfloat16)
    far = pltpu.VMEM((STEPS, GRID, 64, C2), jnp.bfloat16)
    return pl.pallas_call(
        exchange_kernel,
        in_specs=[scalar, anywhere] + [inside] * 5,
        out_specs=[anywhere, anywhere, scalar, anywhere],
        out_shape=[
            jax.ShapeDtypeStruct((2, SIDE, SIDE, GRID, 64, C2), jnp.bfloat16),
            jax.ShapeDtypeStruct((2, SIDE, SIDE, GRID, 128), jnp.float32),
            jax.ShapeDtypeStruct((128,), jnp.int32),
            jax.ShapeDtypeStruct((SIDE * SIDE, GRID, 1, 128), jnp.int32),
        ],
        scratch_shapes=[
            pltpu.VMEM((OWN, 16, 64, 384), jnp.bfloat16),
            pltpu.VMEM((PAIR, GRID, 64, 9 * C1), jnp.bfloat16),
            pltpu.VMEM((STEPS, GRID, PAIR, 64, C2), jnp.bfloat16),
            pltpu.VMEM((STEPS, GRID, PAIR, 64, C2), jnp.bfloat16),
            near,
            near,
            far,
            far,
            pltpu.VMEM((2, SIDE, SIDE, GRID, 64, C2), jnp.bfloat16),
            pltpu.VMEM((STEPS, PAIR, C3), jnp.float32),
            pltpu.VMEM((STEPS, PAIR, C3), jnp.float32),
            pltpu.VMEM((OWN, 128), jnp.float32),
            pltpu.VMEM((GRID, OWN, 128), jnp.float32),
            pltpu.VMEM((2, SIDE, GRID, OWN, 128), jnp.float32),
            pltpu.VMEM((2, SIDE, SIDE, GRID, 128), jnp.float32),
            pltpu.VMEM((1, 128), jnp.int32),
            pltpu.SMEM((SIDE * SIDE, GRID, 1, 128), jnp.int32),
            pltpu.SMEM((OWN,), jnp.int32),
            dma((OWN,)),
            dma((3, GRID)),
            dma((3, GRID)),
            dma((2,)),
            dma((STEPS, GRID)),
            dma((STEPS, GRID)),
            dma((STEPS,)),
            dma((2, STEPS, 2)),
            dma((2, STEPS, 2)),
            dma((2, STEPS, 2)),
            dma((2, STEPS, 2)),
            dma((GRID,)),
            dma((GRID,)),
            dma((1,)),
            dma((2, SIDE)),
            dma((2, SIDE)),
            dma((2,)),
            dma((2, SIDE, SIDE)),
            dma((2, SIDE, SIDE)),
            dma((2, SIDE)),
            dma((2, SIDE)),
            dma((2, SIDE)),
            dma((2,)),
        ],
        compiler_params=pltpu.CompilerParams(vmem_limit_bytes=60 * 2**20, collective_id=0, has_side_effects=True),
        name="exchange",
    )(dest, pixels, embed_w, embed_g, mixing_w, mixing_g, project_w)


def spread_groups(st, base):
    lane = lax.broadcasted_iota(jnp.int32, st.shape, 1)
    return jnp.concatenate(
        [jnp.take_along_axis(st, base + 8 * i + lane // 16, axis=1) for i in range(C3 // 128)], axis=1
    )


PART = 32
PARTS = 256 // PART


def decode_kernel(state, arrived, marks, weight, gain, out, act, ready, rows, st, in_sem, out_sem):
    def fetch(i):
        return pltpu.make_async_copy(arrived.at[:, :, i], act.at[i], in_sem.at[i])

    def put(i):
        return pltpu.make_async_copy(ready.at[i], out.at[pl.ds(i * PART, PART)], out_sem.at[i])

    def begin(i, carry):
        fetch(i).start()
        return carry

    lax.fori_loop(0, PARTS, begin, 0)

    def work(i, carry):
        fetch(i).wait()
        for j in range(16):
            first, number = state[i * 16 + j] % 2, state[i * 16 + j] // 2
            for r in range(CAP):
                which = first if r == 0 else 1 - first
                n = CAP * j + r
                rows[n] = jnp.where(number > r, act[i, which, j], jnp.zeros((64, C2), jnp.bfloat16))
                st[n : n + 1, :] = jnp.where(number > r, marks[which, j, pl.ds(i, 1), :], 0.0)
        mean = spread_groups(st[...], 0)
        scale = spread_groups(st[...], 32) * gain[...]
        for k in range(0, PART, 4):
            values = jnp.dot(rows[k : k + 4].reshape(-1, C2), weight[...], preferred_element_type=jnp.float32)
            for j in range(4):
                n = k + j
                one = (values[64 * j : 64 * j + 64] - mean[n : n + 1]) * scale[n : n + 1]
                ready[i, n] = one.astype(jnp.bfloat16)
        put(i).start()
        return carry

    lax.fori_loop(0, PARTS, work, 0)

    def finish(i, carry):
        put(i).wait()
        return carry

    lax.fori_loop(0, PARTS, finish, 0)


def decode_call(state, arrived, marks, weight, gain):
    anywhere = pl.BlockSpec(memory_space=pl.ANY)
    inside = pl.BlockSpec(memory_space=pltpu.VMEM)
    return pl.pallas_call(
        decode_kernel,
        in_specs=[pl.BlockSpec(memory_space=pltpu.SMEM), anywhere, inside, inside, inside],
        out_specs=anywhere,
        scratch_shapes=[
            pltpu.VMEM((PARTS, 2, 16, 64, C2), jnp.bfloat16),
            pltpu.VMEM((PARTS, PART, 64, C3), jnp.bfloat16),
            pltpu.VMEM((PART, 64, C2), jnp.bfloat16),
            pltpu.VMEM((PART, 128), jnp.float32),
            pltpu.SemaphoreType.DMA((PARTS,)),
            pltpu.SemaphoreType.DMA((PARTS,)),
        ],
        out_shape=jax.ShapeDtypeStruct((256, 64, C3), jnp.bfloat16),
        compiler_params=pltpu.CompilerParams(vmem_limit_bytes=60 * 2**20),
        name="decode",
    )(state, arrived, marks, weight, gain)


def on_device(
    pixels, destination, embed_weight, embed_gain, mixing_weight, mixing_gain, project_weight, project_gain
):
    arrived, marks, state, _ = exchange_call(
        destination.reshape(1, OWN),
        pixels,
        embed_weight,
        embed_gain.reshape(1, C1),
        mixing_weight.reshape(3, 9 * C1, C2),
        mixing_gain.reshape(1, C2),
        project_weight,
    )
    out = decode_call(
        state,
        arrived.reshape(2, 16, GRID, 64, C2),
        marks.reshape(2, 16, GRID, 128),
        project_weight,
        project_gain.reshape(1, C3),
    )
    return out.reshape(256, 8, GRID, C3)


def solution(mesh):
    return jax.shard_map(
        on_device,
        mesh=mesh,
        in_specs=(P(("clip", "patch"), None, None, None), P(("clip", "patch"), None), P(), P(), P(), P(), P(), P()),
        out_specs=P("clip", None, "patch", None),
        check_vma=False,
    )
```

```python
import functools

import jax
import jax.numpy as jnp
from jax import lax
from jax.experimental import pallas as pl
from jax.experimental.pallas import tpu as pltpu
from jax.sharding import PartitionSpec as P

GRID = 8
CAP = 2
OWN = 8
C1, C2, C3 = 128, 256, 512
GROUPS = 32
PAIR = 2
SIDE = 4
STEPS = OWN // PAIR
HI = lax.Precision.HIGHEST
MESH = pl.DeviceIdType.MESH


def fold(rows, size):
    lanes = rows.shape[1]
    lane = lax.broadcasted_iota(jnp.int32, rows.shape, 1)
    step = 1
    while step < size:
        up = pltpu.roll(rows, lanes - step, 1)
        down = pltpu.roll(rows, step, 1)
        rows = rows + jnp.where((lane & step) == 0, up, down)
        step *= 2
    return rows


def group_sums(parts):
    channels = parts[0].shape[1]
    size = channels // GROUPS
    rows = []
    for part in parts:
        total = jnp.sum(part, axis=0, keepdims=True)
        rows += [total[:, i : i + 128] for i in range(0, channels, 128)]
    folded = fold(jnp.concatenate(rows, axis=0), size)
    each = channels // 128
    return [
        jnp.concatenate([folded[n * each + i : n * each + i + 1] for i in range(each)], axis=1)
        for n in range(len(parts))
    ]


def moments(parts):
    rows, channels = parts[0].shape
    inverse = 1.0 / (rows * (channels // GROUPS))
    means = [s * inverse for s in group_sums(parts)]
    squares = []
    for part, mean in zip(parts, means):
        centred = part - mean
        squares.append(centred * centred)
    scales = [lax.rsqrt(s * inverse + 1e-05) for s in group_sums(squares)]
    return means, scales


def silu(v):
    h = 0.5 * v
    return h + h * jnp.tanh(h)


def encode_pair(tubes, embed_w, embed_g, mixing_w, mixing_g, project_w, first, spread, second, act, after):
    for n in range(PAIR):
        wide = jnp.dot(tubes[n], embed_w[...], preferred_element_type=jnp.float32)
        first[n] = wide.reshape(16, GRID, GRID, C1)
    means, scales = moments([first[n].reshape(1024, C1) for n in range(PAIR)])
    place = lax.broadcasted_iota(jnp.int32, (8, GRID, C1), 1)
    for n in range(PAIR):
        gain = scales[n] * embed_g[...]
        for y in range(GRID):
            part = silu((first[n, :, y] - means[n]) * gain).reshape(8, 2, GRID, C1)
            for j in range(3):
                low = j * 3 * C1
                moved = []
                for a in range(2):
                    one = part[:, a]
                    if j == 0:
                        one = jnp.where(place == 0, 0.0, pltpu.roll(one, 1, 1))
                    elif j == 2:
                        one = jnp.where(place == GRID - 1, 0.0, pltpu.roll(one, GRID - 1, 1))
                    moved.append(one)
                prior = jnp.concatenate([jnp.zeros((1, GRID, C1), jnp.float32), moved[1][:-1]], axis=0)
                for a, one in enumerate((prior, moved[0], moved[1])):
                    spread[n, y, :, low + a * C1 : low + (a + 1) * C1] = one.reshape(64, C1).astype(jnp.bfloat16)
        second[n] = jnp.dot(spread[n].reshape(512, 9 * C1), mixing_w[1], preferred_element_type=jnp.float32)
        second[n, 64:512] += jnp.dot(spread[n, 0:7].reshape(448, 9 * C1), mixing_w[0], preferred_element_type=jnp.float32)
        second[n, 0:448] += jnp.dot(spread[n, 1:8].reshape(448, 9 * C1), mixing_w[2], preferred_element_type=jnp.float32)
    for n in range(PAIR):
        (mean,), (scale,) = moments([second[n]])
        gain = scale * mixing_g[...]
        for y in range(GRID):
            act[y, n] = silu((second[n, 64 * y : 64 * y + 64] - mean) * gain).astype(jnp.bfloat16)
    after()
    return moments(
        [jnp.dot(act[:, n].reshape(512, C2), project_w[...], preferred_element_type=jnp.float32) for n in range(PAIR)]
    )


def pick_lanes(mean, scale):
    channel = lax.broadcasted_iota(jnp.int32, (C3, 128), 0)
    lane = lax.broadcasted_iota(jnp.int32, (C3, 128), 1)
    of_mean = ((channel == lane * 16) & (lane < 32)).astype(jnp.float32)
    of_scale = ((channel == (lane - 32) * 16) & (lane >= 32) & (lane < 64)).astype(jnp.float32)
    return jnp.dot(mean, of_mean, precision=HI, preferred_element_type=jnp.float32) + jnp.dot(
        scale, of_scale, precision=HI, preferred_element_type=jnp.float32
    )


class Place:
    def __init__(self):
        self.c, self.p = lax.axis_index("clip"), lax.axis_index("patch")
        self.z, self.x = self.c // SIDE, lax.rem(self.c, SIDE)

    def line(self, which):
        return self.z if which else self.x

    def beside(self, which, by):
        other = lax.rem(self.line(which) + by, SIDE)
        return (other * SIDE + self.x if which else self.z * SIDE + other, self.p), other

    def partner(self, by):
        other = lax.rem(self.p + by, GRID)
        return (self.c, other), other


def exchange_kernel(
    dest, pixels, embed_w, embed_g, mixing_w, mixing_g, project_w,
    arrived, marks, state, names,
    tubes, first, spread, second, act, own, near_x, near_z, far_x, far_z, packed, mean_s, scale_s, tile, tiles, lines, pack_s, name_row, name_s, order,
    pix_sem, send_n, recv_n, keep_n, send_y, recv_y, keep_y, send_g, recv_g, send_f, recv_f, send_s, recv_s, keep_s,
    send_l, recv_l, keep_l, send_r, recv_r, keep_r, send_q, recv_q, keep_q,
):
    me = Place()
    near, far = (near_x, near_z), (far_x, far_z)
    loads = [pltpu.make_async_copy(pixels.at[n], tubes.at[n], pix_sem.at[n]) for n in range(OWN)]
    for load in loads:
        load.start()
    barrier = pltpu.get_barrier_semaphore()
    for by in range(1, GRID):
        pl.semaphore_signal(barrier, inc=1, device_id=me.partner(by)[0], device_id_type=MESH)
    for which in range(2):
        for by in range(1, SIDE):
            pl.semaphore_signal(barrier, inc=1, device_id=me.beside(which, by)[0], device_id_type=MESH)

    d = [dest[0, k] for k in range(OWN)]
    at = []
    for k in range(OWN):
        ahead = [((d[j] <= d[k]) if j < k else (d[j] < d[k])).astype(jnp.int32) for j in range(OWN) if j != k]
        at.append(functools.reduce(lambda a, b: a + b, ahead))
    lane = lax.broadcasted_iota(jnp.int32, (1, 128), 1)
    row = jnp.zeros((1, 128), jnp.int32)
    for s in range(OWN):
        hit = [(at[k] == s).astype(jnp.int32) for k in range(OWN)]
        order[s] = functools.reduce(lambda a, b: a + b, [hit[k] * k for k in range(OWN)])
        name = functools.reduce(lambda a, b: a + b, [hit[k] * d[k] for k in range(OWN)])
        row = jnp.where(lane == s, name, row)
    name_row[...] = row
    pl.semaphore_wait(barrier, GRID - 1 + 2 * (SIDE - 1))

    def remote(src, dst, send, recv, device):
        return pltpu.make_async_remote_copy(
            src_ref=src, dst_ref=dst, send_sem=send, recv_sem=recv, device_id=device, device_id_type=MESH
        )

    def name_y(by, incoming):
        device, other = me.partner(by)
        to = other if incoming else me.p
        return remote(name_row, names.at[me.c, to], send_n.at[0, by], recv_n.at[0, to], device)

    def name_x(by, incoming):
        device, other = me.beside(0, by)
        to = other if incoming else me.x
        return remote(names.at[me.c], names.at[me.z * SIDE + to], send_n.at[1, by], recv_n.at[1, to], device)

    def name_z(by, incoming):
        device, other = me.beside(1, by)
        to = other if incoming else me.z
        mine = names.at[pl.ds(me.z * SIDE, SIDE)]
        return remote(mine, names.at[pl.ds(to * SIDE, SIDE)], send_n.at[2, by], recv_n.at[2, to], device)

    keep_name = pltpu.make_async_copy(name_row, names.at[me.c, me.p], keep_n.at[0])
    keep_name.start()
    for by in range(1, GRID):
        name_y(by, False).start()
    for load in loads:
        load.wait()

    def across(m, by):
        device, other = me.partner(by)
        return remote(act.at[m, other], own.at[m, me.p], send_y.at[m, by], recv_y.at[m, me.p], device)

    def across_in(m, by):
        device, other = me.partner(by)
        return remote(act.at[m, other], own.at[m, other], send_y.at[m, by], recv_y.at[m, other], device)

    def kept(m):
        return pltpu.make_async_copy(act.at[m, me.p], own.at[m, me.p], keep_y.at[m])

    def gather(which, m, way):
        device, _ = me.beside(which, 1 if way == 0 else SIDE - 1)
        return remote(
            own.at[m, :, which], near[which].at[way, m], send_g.at[which, m, way], recv_g.at[which, m, way], device
        )

    def pass_on(which, m, way):
        device, _ = me.beside(which, 1 if way == 0 else SIDE - 1)
        part = pl.ds(way * 4, 4)
        return remote(
            near[which].at[way, m, part], far[which].at[m, part], send_f.at[which, m, way], recv_f.at[which, m, way], device
        )

    both = [(which, way) for which in range(2) for way in range(2)]

    def start_across(m):
        for by in range(1, GRID):
            across(m, by).start()
        kept(m).start()

    def start_gather(m):
        kept(m).wait()
        for by in range(1, GRID):
            across_in(m, by).wait_recv()
        for which, way in both:
            gather(which, m, way).start()

    def start_pass(m):
        for which, way in both:
            gather(which, m, way).wait_recv()
            pass_on(which, m, way).start()

    def encode(m):
        def after():
            start_across(m)

            @pl.when(m == 0)
            def _():
                keep_name.wait()
                for by in range(1, GRID):
                    name_y(by, True).wait_recv()
                for by in range(1, SIDE):
                    name_x(by, False).start()

            @pl.when(m >= 1)
            def _():
                start_gather(m - 1)

            @pl.when(m == 1)
            def _():
                for by in range(1, SIDE):
                    name_x(by, True).wait_recv()
                for by in range(1, SIDE):
                    name_z(by, False).start()

            @pl.when(m >= 2)
            def _():
                start_pass(m - 2)

        values = [tubes[order[PAIR * m + n]].reshape(1024, 384) for n in range(PAIR)]
        means, scales = encode_pair(
            values, embed_w, embed_g, mixing_w, mixing_g, project_w, first, spread, second, act.at[m], after
        )
        for n in range(PAIR):
            mean_s[m, n : n + 1] = means[n]
            scale_s[m, n : n + 1] = scales[n]

    def loop(m, carry):
        encode(m)
        return carry

    lax.fori_loop(0, STEPS, loop, 0)

    def stat_y(by, incoming):
        device, other = me.partner(by)
        to = other if incoming else me.p
        return remote(tile, tiles.at[to], send_s.at[by], recv_s.at[to], device)

    def stat_line(which, by, incoming):
        device, other = me.beside(which, by)
        to = other if incoming else me.line(which)
        return remote(tiles, lines.at[which, to], send_l.at[which, by], recv_l.at[which, to], device)

    mean = mean_s[...].reshape(OWN, C3)
    scale = scale_s[...].reshape(OWN, C3)
    tile[...] = pick_lanes(mean, scale)
    for by in range(1, GRID):
        stat_y(by, False).start()
    keep_tile = pltpu.make_async_copy(tile, tiles.at[me.p], keep_s.at[0])
    keep_tile.start()
    start_gather(STEPS - 1)
    for by in range(1, SIDE):
        name_z(by, True).wait_recv()
    fetch_names = pltpu.make_async_copy(names, name_s, keep_n.at[1])
    fetch_names.start()
    start_pass(STEPS - 2)
    keep_tile.wait()
    for by in range(1, GRID):
        stat_y(by, True).wait_recv()
    for which in range(2):
        for by in range(1, SIDE):
            stat_line(which, by, False).start()
        pltpu.make_async_copy(tiles, lines.at[which, me.line(which)], keep_l.at[which]).start()
    def target(which, line, s):
        return arrived.at[1, s, line] if which else arrived.at[0, line, s]

    def mark(which, line):
        return marks.at[1, :, line] if which else marks.at[0, line]

    def source(which, kind):
        return lax.rem(me.line(which) + (0, SIDE - 1, 1, 2)[kind], SIDE)

    def route(which, by, kind, incoming):
        device, other = me.beside(1 - which, by)
        to, s = other if incoming else me.line(1 - which), source(which, kind)
        return remote(
            packed.at[which, other, s], target(which, to, s), send_r.at[which, by, kind], recv_r.at[which, to, kind], device
        )

    def route_mark(which, by, incoming):
        device, other = me.beside(1 - which, by)
        to = other if incoming else me.line(1 - which)
        return remote(
            pack_s.at[which, other], mark(which, to), send_q.at[which, by], recv_q.at[which, to], device
        )

    def stay_route(which, kind):
        line, s = me.line(1 - which), source(which, kind)
        return pltpu.make_async_copy(packed.at[which, line, s], target(which, line, s), keep_r.at[which, kind])

    def stay_mark(which):
        line = me.line(1 - which)
        return pltpu.make_async_copy(pack_s.at[which, line], mark(which, line), keep_q.at[which])

    def find(which, other, s, p):
        owner = s * SIDE + me.x if which else me.z * SIDE + s
        wanted = me.z * SIDE + other if which else other * SIDE + me.x
        m = jnp.int32(0)
        for k in range(STEPS):
            m = jnp.where(name_s[owner, p, 0, PAIR * k + which] == wanted, k, m)
        return m

    def pack(which, other, kind):
        s = source(which, kind)

        def one(p, carry):
            m = find(which, other, s, p)
            if kind == 0:
                packed[which, other, s, p] = own[m, p, which]
            elif kind == 3:
                packed[which, other, s, p] = far[which][m, p]
            else:
                packed[which, other, s, p] = near[which][kind - 1, m, p]
            return carry

        lax.fori_loop(0, GRID, one, 0)

    def start_route(kinds, hops):
        for by in hops:
            for which in range(2):
                for kind in kinds:
                    _, other = me.beside(1 - which, by)
                    pack(which, other, kind)
                    if by:
                        route(which, by, kind, False).start()
                    else:
                        stay_route(which, kind).start()

    def pack_mark(which, other):
        def one(s, carry):
            for p in range(GRID):
                m = find(which, other, s, p)
                pack_s[which, other, s, p : p + 1, :] = lines[which, s, p, pl.ds(PAIR * m + which, 1), :]
            return carry

        lax.fori_loop(0, SIDE, one, 0)

    fetch_names.wait()
    start_route((0,), (2, 1, 3))
    start_pass(STEPS - 1)
    start_route((1, 2), (2, 1, 3))
    for m in range(STEPS):
        for which, way in both:
            pass_on(which, m, way).wait_recv()
    start_route((3,), (2, 1, 3))
    start_route((0, 1, 2, 3), (0,))
    for which in range(2):
        pltpu.make_async_copy(tiles, lines.at[which, me.line(which)], keep_l.at[which]).wait()
        for by in range(1, SIDE):
            stat_line(which, by, True).wait_recv()
    for by in (2, 1, 3, 0):
        for which in range(2):
            _, other = me.beside(1 - which, by)
            pack_mark(which, other)
            if by:
                route_mark(which, by, False).start()
            else:
                stay_mark(which).start()

    def count(i, carry):
        c, p = lax.rem(i, SIDE * SIDE), i // (SIDE * SIDE)
        before, number = jnp.int32(0), jnp.int32(0)
        for k in range(OWN):
            name = name_s[c, p, 0, k]
            before = before + (name < me.c).astype(jnp.int32)
            number = number + (name == me.c).astype(jnp.int32)
        state[i] = before % 2 + 2 * number
        return carry

    lax.fori_loop(0, GRID * SIDE * SIDE, count, 0)

    def drain(m, carry):
        for by in range(1, GRID):
            across(m, by).wait_send()
        for which, way in both:
            gather(which, m, way).wait_send()
            pass_on(which, m, way).wait_send()
        return carry

    lax.fori_loop(0, STEPS, drain, 0)
    for by in range(1, GRID):
        name_y(by, False).wait_send()
        stat_y(by, False).wait_send()
    for by in range(1, SIDE):
        name_x(by, False).wait_send()
        name_z(by, False).wait_send()
        for which in range(2):
            stat_line(which, by, False).wait_send()
    for which in range(2):
        stay_mark(which).wait()
        for kind in range(SIDE):
            stay_route(which, kind).wait()
            for by in range(1, SIDE):
                route(which, by, kind, True).wait_recv()
                route(which, by, kind, False).wait_send()
        for by in range(1, SIDE):
            route_mark(which, by, True).wait_recv()
            route_mark(which, by, False).wait_send()


def exchange_call(dest, pixels, embed_w, embed_g, mixing_w, mixing_g, project_w):
    anywhere = pl.BlockSpec(memory_space=pl.ANY)
    inside = pl.BlockSpec(memory_space=pltpu.VMEM)
    scalar = pl.BlockSpec(memory_space=pltpu.SMEM)
    dma = pltpu.SemaphoreType.DMA
    near = pltpu.VMEM((2, STEPS, GRID, 64, C2), jnp.bfloat16)
    far = pltpu.VMEM((STEPS, GRID, 64, C2), jnp.bfloat16)
    return pl.pallas_call(
        exchange_kernel,
        in_specs=[scalar, anywhere] + [inside] * 5,
        out_specs=[anywhere, anywhere, scalar, anywhere],
        out_shape=[
            jax.ShapeDtypeStruct((2, SIDE, SIDE, GRID, 64, C2), jnp.bfloat16),
            jax.ShapeDtypeStruct((2, SIDE, SIDE, GRID, 128), jnp.float32),
            jax.ShapeDtypeStruct((128,), jnp.int32),
            jax.ShapeDtypeStruct((SIDE * SIDE, GRID, 1, 128), jnp.int32),
        ],
        scratch_shapes=[
            pltpu.VMEM((OWN, 16, 64, 384), jnp.bfloat16),
            pltpu.VMEM((PAIR, 16, GRID, GRID, C1), jnp.float32),
            pltpu.VMEM((PAIR, GRID, 64, 9 * C1), jnp.bfloat16),
            pltpu.VMEM((PAIR, 512, C2), jnp.float32),
            pltpu.VMEM((STEPS, GRID, PAIR, 64, C2), jnp.bfloat16),
            pltpu.VMEM((STEPS, GRID, PAIR, 64, C2), jnp.bfloat16),
            near,
            near,
            far,
            far,
            pltpu.VMEM((2, SIDE, SIDE, GRID, 64, C2), jnp.bfloat16),
            pltpu.VMEM((STEPS, PAIR, C3), jnp.float32),
            pltpu.VMEM((STEPS, PAIR, C3), jnp.float32),
            pltpu.VMEM((OWN, 128), jnp.float32),
            pltpu.VMEM((GRID, OWN, 128), jnp.float32),
            pltpu.VMEM((2, SIDE, GRID, OWN, 128), jnp.float32),
            pltpu.VMEM((2, SIDE, SIDE, GRID, 128), jnp.float32),
            pltpu.VMEM((1, 128), jnp.int32),
            pltpu.SMEM((SIDE * SIDE, GRID, 1, 128), jnp.int32),
            pltpu.SMEM((OWN,), jnp.int32),
            dma((OWN,)),
            dma((3, GRID)),
            dma((3, GRID)),
            dma((2,)),
            dma((STEPS, GRID)),
            dma((STEPS, GRID)),
            dma((STEPS,)),
            dma((2, STEPS, 2)),
            dma((2, STEPS, 2)),
            dma((2, STEPS, 2)),
            dma((2, STEPS, 2)),
            dma((GRID,)),
            dma((GRID,)),
            dma((1,)),
            dma((2, SIDE)),
            dma((2, SIDE)),
            dma((2,)),
            dma((2, SIDE, SIDE)),
            dma((2, SIDE, SIDE)),
            dma((2, SIDE)),
            dma((2, SIDE)),
            dma((2, SIDE)),
            dma((2,)),
        ],
        compiler_params=pltpu.CompilerParams(vmem_limit_bytes=60 * 2**20, collective_id=0, has_side_effects=True),
        name="exchange",
    )(dest, pixels, embed_w, embed_g, mixing_w, mixing_g, project_w)


def spread_groups(st, base):
    lane = lax.broadcasted_iota(jnp.int32, st.shape, 1)
    return jnp.concatenate(
        [jnp.take_along_axis(st, base + 8 * i + lane // 16, axis=1) for i in range(C3 // 128)], axis=1
    )


PART = 32
PARTS = 256 // PART


def decode_kernel(state, arrived, marks, weight, gain, out, act, ready, rows, st, in_sem, out_sem):
    def fetch(i):
        return pltpu.make_async_copy(arrived.at[:, :, i], act.at[i], in_sem.at[i])

    def put(i):
        return pltpu.make_async_copy(ready.at[i], out.at[pl.ds(i * PART, PART)], out_sem.at[i])

    def begin(i, carry):
        fetch(i).start()
        return carry

    lax.fori_loop(0, PARTS, begin, 0)

    def work(i, carry):
        fetch(i).wait()
        for j in range(16):
            first, number = state[i * 16 + j] % 2, state[i * 16 + j] // 2
            for r in range(CAP):
                which = first if r == 0 else 1 - first
                n = CAP * j + r
                rows[n] = jnp.where(number > r, act[i, which, j], jnp.zeros((64, C2), jnp.bfloat16))
                st[n : n + 1, :] = jnp.where(number > r, marks[which, j, pl.ds(i, 1), :], 0.0)
        mean = spread_groups(st[...], 0)
        scale = spread_groups(st[...], 32) * gain[...]
        for k in range(0, PART, 4):
            values = jnp.dot(rows[k : k + 4].reshape(-1, C2), weight[...], preferred_element_type=jnp.float32)
            for j in range(4):
                n = k + j
                one = (values[64 * j : 64 * j + 64] - mean[n : n + 1]) * scale[n : n + 1]
                ready[i, n] = one.astype(jnp.bfloat16)
        put(i).start()
        return carry

    lax.fori_loop(0, PARTS, work, 0)

    def finish(i, carry):
        put(i).wait()
        return carry

    lax.fori_loop(0, PARTS, finish, 0)


def decode_call(state, arrived, marks, weight, gain):
    anywhere = pl.BlockSpec(memory_space=pl.ANY)
    inside = pl.BlockSpec(memory_space=pltpu.VMEM)
    return pl.pallas_call(
        decode_kernel,
        in_specs=[pl.BlockSpec(memory_space=pltpu.SMEM), anywhere, inside, inside, inside],
        out_specs=anywhere,
        scratch_shapes=[
            pltpu.VMEM((PARTS, 2, 16, 64, C2), jnp.bfloat16),
            pltpu.VMEM((PARTS, PART, 64, C3), jnp.bfloat16),
            pltpu.VMEM((PART, 64, C2), jnp.bfloat16),
            pltpu.VMEM((PART, 128), jnp.float32),
            pltpu.SemaphoreType.DMA((PARTS,)),
            pltpu.SemaphoreType.DMA((PARTS,)),
        ],
        out_shape=jax.ShapeDtypeStruct((256, 64, C3), jnp.bfloat16),
        compiler_params=pltpu.CompilerParams(vmem_limit_bytes=60 * 2**20),
        name="decode",
    )(state, arrived, marks, weight, gain)


def on_device(
    pixels, destination, embed_weight, embed_gain, mixing_weight, mixing_gain, project_weight, project_gain
):
    arrived, marks, state, _ = exchange_call(
        destination.reshape(1, OWN),
        pixels,
        embed_weight,
        embed_gain.reshape(1, C1),
        mixing_weight.reshape(3, 9 * C1, C2),
        mixing_gain.reshape(1, C2),
        project_weight,
    )
    out = decode_call(
        state,
        arrived.reshape(2, 16, GRID, 64, C2),
        marks.reshape(2, 16, GRID, 128),
        project_weight,
        project_gain.reshape(1, C3),
    )
    return out.reshape(256, 8, GRID, C3)


def solution(mesh):
    return jax.shard_map(
        on_device,
        mesh=mesh,
        in_specs=(P(("clip", "patch"), None, None, None), P(("clip", "patch"), None), P(), P(), P(), P(), P(), P()),
        out_specs=P("clip", None, "patch", None),
        check_vma=False,
    )
```
